256 devices in a mesh: occ: 4 (over z_hi), vir: 64 (over y, z_lo, x, core).
Axes of the slice: x: 4, y: 4, z: 8 (z_hi: 4, z_lo: 2; z = z_hi * 2 + z_lo), core: 2. Of those that a mesh axis runs over, the one named last changes fastest.
Arguments:
- amplitudes: float32 [49152, 1024], P('vir', 'occ'), may hold values from -6 to 6
- integrals: float32 [768, 327680], P('occ', 'vir'), may hold values from -0.21875 to 0.21875
- eps_vir: float32 [327680], P('vir'), may hold values from 0.5 to 3
- eps_occ: float32 [1024], P('occ'), may hold values from -2 to -0.5
- panel_owner: int32 [12], replicated, may hold values from 0 to 63
- block_target: int32 [4096], replicated, may hold values from 0 to 4095, as said below
Outputs:
- ladder_tiles: float32 [327680, 1024], P('vir', 'occ')
The draws below stay inside these ranges and needn't reach their ends.
Inputs may be any that keep to these rules, and one draw needn't show every extreme that they name: block_target is a permutation. The 64 blocks of each index of vir go to 32 owner indices, exactly 2 to each, and each owner receives exactly 2 blocks from each of 32 senders; block b of the whole lies on index b // 64.
All inputs are finite; a program needn't handle non-finite values.
Results may differ from the reference program's by a relative error of at most 0.000082.
Values sent between devices are 32-bit elements; how exact they have to be, the bound alone decides.
A program may use at most 128 MiB of HBM per device.

```python
import jax
import jax.numpy as jnp
from jax import lax

PANEL = 64
STEPS = 12
VP_DEV = 5120
NB_DEV = 64
SP = 768
VP = 327680
OP = 1024
NBLK = 4096
BLK = 80
AROWS = 49152
N_VIR = 64


def draw_block_target(key, part):
    devices = NBLK // NB_DEV
    capacity = max(2, 2 * NB_DEV // devices)
    rounds = NB_DEV // capacity
    key_shift, key_order, key_slot = jax.random.split(key, 3)
    shifts = jax.random.permutation(key_shift, devices)[:rounds]
    orders = jax.vmap(lambda sub_key: jax.random.permutation(sub_key, NB_DEV))(jax.random.split(key_order, devices))
    slotting = jax.vmap(lambda sub_key: jax.random.permutation(sub_key, NB_DEV))(jax.random.split(key_slot, devices))
    round_of = orders // capacity
    within = orders % capacity
    senders = jnp.arange(devices)[:, None]
    owner = (senders + shifts[round_of]) % devices
    slot = slotting[owner, round_of * capacity + within]
    return (owner * NB_DEV + slot).reshape(-1).astype(jnp.int32)


def set_ends(values, own_key, least, top_value):
    dims = values.shape
    index_at = [jax.random.randint(jax.random.fold_in(own_key, axis), (), 0, dims[axis]) for axis in range(len(dims))]
    values = values.at[tuple(index_at)].set(least)
    longest = dims.index(max(dims))
    index_at[longest] = (index_at[longest] + 1) % dims[longest]
    return values.at[tuple(index_at)].set(top_value)


def levels(rng, shape, cuts, least, top_value):
    def one(position, blocks):
        draws = jax.random.uniform(jax.random.fold_in(jax.random.fold_in(rng, 6), position), (blocks,), jnp.float32, least / len(cuts), top_value / len(cuts))
        return jnp.repeat(jnp.exp(draws), shape[position] // blocks).reshape((-1,) + (1,) * (len(shape) - position - 1))

    level = one(*cuts[0])
    for cut in cuts[1:]:
        level = level * one(*cut)
    return level


def normal_values(key, dims, deviation, bound, pieces=(), dtype=jnp.bfloat16):
    entries = deviation * jax.random.normal(key, dims, jnp.float32)
    if pieces:
        entries = entries * levels(key, dims, pieces, -0.22, 0.18)
    return jnp.clip(entries, -bound, bound).astype(dtype)


def setup_inputs(seed: int = 0) -> dict:
    key_of = jax.random.split(jax.random.key(seed), 7)
    return {
        "amplitudes": normal_values(key_of[0], (AROWS, OP), 1.0, 6.0, ((0, 64), (1, 4)), jnp.float32),
        "integrals": normal_values(key_of[1], (SP, VP), SP ** -0.5, 0.21875, ((0, 4), (1, 64)), jnp.float32),
        "eps_vir": jnp.clip(0.5 + 2.5 * jax.random.uniform(key_of[2], (VP,), jnp.float32) ** levels(key_of[2], (VP,), ((0, 64),), -0.2, 0.2), 0.5, 3.0),
        "eps_occ": jnp.clip(-2.0 + 1.5 * jax.random.uniform(key_of[3], (OP,), jnp.float32) ** levels(key_of[3], (OP,), ((0, 4),), -0.2, 0.2), -2.0, -0.5),
        "panel_owner": set_ends(jax.random.randint(key_of[4], (STEPS,), 0, N_VIR), jax.random.fold_in(key_of[4], 1), 0, N_VIR - 1).astype(jnp.int32),
        "block_target": draw_block_target(jax.random.fold_in(key_of[6], 71), 0),
    }


def reference(amplitudes, integrals, eps_vir, eps_occ, panel_owner, block_target):
    picked = []
    for step_index in range(STEPS):
        first_row = ((panel_owner[step_index] * STEPS + step_index) * PANEL).astype(jnp.int32)
        picked.append(lax.dynamic_slice_in_dim(amplitudes, first_row, PANEL, 0))
    panels = jnp.concatenate(picked, 0)
    grouped = integrals.reshape(SP, N_VIR, VP_DEV).transpose(1, 0, 2)
    energies = eps_vir.reshape(N_VIR, VP_DEV)

    def one_group(pair_args):
        group_ints, group_eps = pair_args
        ladder = lax.dot_general(group_ints, panels, (((0,), (0,)), ((), ())),
                                 precision=lax.Precision.HIGHEST, preferred_element_type=jnp.float32)
        return ladder / (group_eps[:, None] - eps_occ[None, :])

    scaled = lax.map(one_group, (grouped, energies))
    blocks = scaled.reshape(NBLK, BLK, OP)
    placed = jnp.zeros_like(blocks).at[block_target].set(blocks)
    return placed.reshape(VP, OP)
```

```python
import functools

import jax
import jax.numpy as jnp
from jax import lax
from jax.experimental import pallas as pl
from jax.experimental.pallas import tpu as pltpu
from jax.sharding import PartitionSpec as P

MESH = pl.DeviceIdType.MESH
STEPS = 12
N_OCC = 4
DIGITS = ((1, 2), (2, 4), (8, 2), (16, 4))


def remote(src, dst, sems, k, peer):
    send, recv = sems
    return pltpu.make_async_remote_copy(
        src_ref=src, dst_ref=dst, send_sem=send.at[k], recv_sem=recv.at[k], device_id=peer, device_id_type=MESH
    )


def gcd16(n):
    g = 16
    while n % g:
        g //= 2
    return g


def panel_kernel(digits, per_step, owner_ref, amp_ref, out_ref, *scratch):
    levels = len(digits)
    arrived, kept, transit = scratch[:levels], scratch[levels : 2 * levels - 1], scratch[2 * levels - 1]
    sems = scratch[2 * levels :]
    occ, vir = lax.axis_index("occ"), lax.axis_index("vir")
    mine = [(vir // stride) % size for stride, size in digits]

    def along(level, digit):
        stride, _ = digits[level]
        return (occ, vir + (digit - mine[level]) * stride)

    up, down = (lax.rem(occ + 1, N_OCC), vir), (lax.rem(occ + N_OCC - 1, N_OCC), vir)
    far = lax.rem(occ + 2, N_OCC)
    peers = [up, down]
    for level, (_, size) in enumerate(digits):
        peers += [along(level, lax.rem(mine[level] + d, size)) for d in range(1, size)]
    barrier = pltpu.get_barrier_semaphore()
    for peer in peers:
        pl.semaphore_signal(barrier, inc=1, device_id=peer, device_id_type=MESH)
    pl.semaphore_wait(barrier, len(peers))

    k = 0
    started = []
    current, base, bases, lengths = amp_ref, 0, [], []
    length = amp_ref.shape[0]
    for level, (stride, size) in enumerate(digits):
        part = length // size
        copies = []
        for d in range(1, size):
            digit = lax.rem(mine[level] + d, size)
            copies.append(
                remote(current.at[pl.ds(digit * part, part)], arrived[level].at[d - 1], sems, k, along(level, digit))
            )
            k += 1
        for copy in copies:
            copy.start()
        offset = mine[level] * part
        base = base + offset
        target, target_base = (kept[level], 0) if level < levels - 1 else (out_ref.at[occ], base)
        for copy in copies:
            copy.wait_recv()
        group = min(gcd16(part), per_step)
        for g in range(part // group):
            holder = owner_ref[(base + g * group) // per_step]
            digit = (holder // stride) % size
            value = current[pl.ds(offset + g * group, group)]
            for d in range(1, size):
                source = lax.rem(mine[level] + size - d, size)
                value = jnp.where(digit == source, arrived[level][d - 1, pl.ds(g * group, group)], value)
            target[pl.ds(target_base + g * group, group)] = value
        started += copies
        current, length = (target, part)
        bases.append(base)
        lengths.append(part)

    for level in range(levels - 1, 0, -1):
        piece = out_ref.at[occ, pl.ds(bases[level], lengths[level])]
        copies = []
        for d in range(1, digits[level][1]):
            digit = lax.rem(mine[level] + d, digits[level][1])
            copies.append(remote(piece, piece, sems, k, along(level, digit)))
            k += 1
        for copy in copies:
            copy.start()
        for copy in copies:
            copy.wait_recv()
        started += copies

    half = lengths[0]
    quarter = half // 2
    sibling = along(0, 1 - mine[0])
    above, below = lax.rem(occ + 1, N_OCC), lax.rem(occ + N_OCC - 1, N_OCC)

    def rows(which, start, size):
        return out_ref.at[which, pl.ds(bases[0] + start, size)]

    own = rows(occ, 0, half)
    first = [
        remote(own, own, sems, k, up),
        remote(own, own, sems, k + 1, down),
        remote(rows(occ, 0, quarter), transit.at[0], sems, k + 2, up),
        remote(rows(occ, quarter, quarter), transit.at[1], sems, k + 3, down),
    ]
    relays = [
        remote(transit.at[0], rows(below, 0, quarter), sems, k + 4, up),
        remote(transit.at[1], rows(above, quarter, quarter), sems, k + 5, down),
    ]
    k += 6
    order = [first[2], first[3], first[0], first[1]]
    for copy in order:
        copy.start()
    shares = [remote(rows(which, 0, half), rows(which, 0, half), sems, k + n, sibling)
              for n, which in enumerate((occ, below, above, far))]
    shares[0].start()
    for n in range(2):
        first[2 + n].wait_recv()
        relays[n].start()
    for n in range(2):
        first[n].wait_recv()
        shares[1 + n].start()
    for n in range(2):
        relays[n].wait_recv()
    shares[3].start()
    for copy in shares:
        copy.wait_recv()
    for copy in started + first + relays + shares:
        copy.wait_send()


def broadcast_panels(amplitudes, panel_owner, digits):
    rows, cols = amplitudes.shape
    units = (rows // 8) * (cols // 128)
    amps = amplitudes.reshape(rows // 8, 8, cols // 128, 128).transpose(0, 2, 1, 3).reshape(units, 8, 128)
    per_step = units // STEPS
    arrived, kept, length, count = [], [], units, 0
    for level, (_, size) in enumerate(digits):
        length //= size
        arrived.append(pltpu.VMEM((size - 1, length, 8, 128), jnp.float32))
        kept.append(pltpu.VMEM((length, 8, 128), jnp.float32))
        count += (size - 1) * (2 if level else 1)
    half = units // digits[0][1]
    count += 10
    out = pl.pallas_call(
        functools.partial(panel_kernel, digits, per_step),
        out_shape=jax.ShapeDtypeStruct((N_OCC, units, 8, 128), jnp.float32),
        in_specs=[pl.BlockSpec(memory_space=pltpu.SMEM), pl.BlockSpec(memory_space=pltpu.VMEM)],
        out_specs=pl.BlockSpec(memory_space=pltpu.VMEM),
        scratch_shapes=arrived
        + kept[:-1]
        + [
            pltpu.VMEM((2, half // 2, 8, 128), jnp.float32),
            pltpu.SemaphoreType.DMA((count,)),
            pltpu.SemaphoreType.DMA((count,)),
        ],
        compiler_params=pltpu.CompilerParams(collective_id=0, has_side_effects=True),
        name="panels",
    )(panel_owner, amps)
    out = out.reshape(N_OCC, rows // 8, cols // 128, 8, 128).transpose(1, 3, 0, 2, 4)
    return out.reshape(rows, N_OCC * cols)


AHEAD = 3


def ladder_kernel(x_ref, high_ref, low_ref, out_ref, held, passing, result, passing_result, send, recv, own_sem):
    chunks = held.shape[1]
    rows, lanes = held.shape[2], held.shape[3]
    width = out_ref.shape[2]
    half, cols = rows // 2, out_ref.shape[1]
    block = cols // 2
    occ, vir = lax.axis_index("occ"), lax.axis_index("vir")
    above, below, far = (lax.rem(occ + n, N_OCC) for n in (1, N_OCC - 1, 2))
    up, down = (above, vir), (below, vir)

    barrier = pltpu.get_barrier_semaphore()
    for peer in (up, down):
        pl.semaphore_signal(barrier, inc=1, device_id=peer, device_id_type=MESH)
    pl.semaphore_wait(barrier, 2)

    def copy(kind, j):
        make = lambda src, dst, peer: pltpu.make_async_remote_copy(
            src_ref=src, dst_ref=dst, send_sem=send.at[kind, j], recv_sem=recv.at[kind, j], device_id=peer,
            device_id_type=MESH,
        )
        if kind == 0:
            return make(x_ref.at[far * chunks + j, pl.ds(0, half)], passing.at[0, j], up)
        if kind == 1:
            return make(x_ref.at[far * chunks + j, pl.ds(half, half)], passing.at[1, j], down)
        if kind == 2:
            return make(x_ref.at[above * chunks + j], held.at[occ, j], up)
        if kind == 3:
            return make(x_ref.at[below * chunks + j], held.at[occ, j], down)
        if kind == 4:
            return make(passing.at[0, j], held.at[below, j, pl.ds(0, half)], up)
        if kind == 5:
            return make(passing.at[1, j], held.at[above, j, pl.ds(half, half)], down)
        if kind == 6:
            return make(result.at[j, far, pl.ds(0, block)], passing_result.at[0, j], up)
        if kind == 7:
            return make(result.at[j, far, pl.ds(block, block)], passing_result.at[1, j], down)
        if kind == 8:
            return make(result.at[j, above], out_ref.at[occ * chunks + j], up)
        if kind == 9:
            return make(result.at[j, below], out_ref.at[occ * chunks + j], down)
        if kind == 10:
            return make(passing_result.at[0, j], out_ref.at[below * chunks + j, pl.ds(0, block)], up)
        return make(passing_result.at[1, j], out_ref.at[above * chunks + j, pl.ds(block, block)], down)

    own_copy = pltpu.make_async_copy(x_ref.at[pl.ds(occ * chunks, chunks)], held.at[occ], own_sem)
    own_copy.start()

    def send_chunk(j):
        for kind in range(4):
            copy(kind, j).start()

    def first(j, _):
        send_chunk(j)
        return 0

    lax.fori_loop(0, AHEAD, first, 0)
    own_copy.wait()

    def compute(j):
        low_lane = lax.broadcasted_iota(jnp.int32, (block, lanes), 1) < lanes // 2
        tiles = [held[n, j, pl.ds(0, cols)] for n in range(N_OCC)]
        folds = [held[n, j, pl.ds(cols, block)] for n in range(N_OCC)]
        for n in range(0, N_OCC, 2):
            left, right = folds[n], folds[n + 1]
            one = jnp.where(low_lane, left, pltpu.roll(right, lanes // 2, 1))
            two = jnp.where(low_lane, pltpu.roll(left, lanes // 2, 1), right)
            tiles.append(jnp.concatenate([one, two], axis=0))
        whole = jnp.concatenate(tiles, axis=1)
        high = whole.astype(jnp.bfloat16)
        low = (whole - high.astype(jnp.float32)).astype(jnp.bfloat16)
        for n in range(N_OCC):
            at = slice(n * width, (n + 1) * width)
            dot = lambda a, b: jnp.dot(a, b, preferred_element_type=jnp.float32)
            result[j, n] = (
                dot(high, low_ref[:, at]) + dot(low, high_ref[:, at])
            ) + dot(high, high_ref[:, at])
        out_ref[occ * chunks + j] = result[j, occ]

    def step(t, _):
        @pl.when(t + AHEAD < chunks)
        def _():
            send_chunk(t + AHEAD)

        @pl.when(t < chunks)
        def _():
            for kind in range(2):
                copy(kind, t).wait_recv()
                copy(4 + kind, t).start()

        @pl.when((t >= 2) & (t < chunks + 2))
        def _():
            for kind in range(6, 10):
                copy(kind, t - 2).start()

        @pl.when((t >= 1) & (t < chunks + 1))
        def _():
            for kind in range(2, 6):
                copy(kind, t - 1).wait_recv()
            compute(t - 1)

        @pl.when(t >= 3)
        def _():
            for kind in range(2):
                copy(6 + kind, t - 3).wait_recv()
                copy(10 + kind, t - 3).start()

        return 0

    lax.fori_loop(0, chunks + 3, step, 0)

    def last(j, _):
        for kind in range(8, 12):
            copy(kind, j).wait_recv()
        for kind in range(12):
            copy(kind, j).wait_send()
        return 0

    lax.fori_loop(0, chunks, last, 0)


def ladder_of(x, high, low):
    pairs, rows, lanes = x.shape
    chunks = pairs // N_OCC
    width = high.shape[1] // N_OCC
    cols = rows * 2 // 3
    vmem = pl.BlockSpec(memory_space=pltpu.VMEM)
    return pl.pallas_call(
        ladder_kernel,
        out_shape=jax.ShapeDtypeStruct((pairs, cols, width), jnp.float32),
        in_specs=[vmem] * 3,
        out_specs=vmem,
        scratch_shapes=[
            pltpu.VMEM((N_OCC, chunks, rows, lanes), jnp.float32),
            pltpu.VMEM((2, chunks, rows // 2, lanes), jnp.float32),
            pltpu.VMEM((chunks, N_OCC, cols, width), jnp.float32),
            pltpu.VMEM((2, chunks, cols // 2, width), jnp.float32),
            pltpu.SemaphoreType.DMA((12, chunks)),
            pltpu.SemaphoreType.DMA((12, chunks)),
            pltpu.SemaphoreType.DMA,
        ],
        compiler_params=pltpu.CompilerParams(collective_id=1, has_side_effects=True),
        name="ladder",
    )(x, high, low)


def split(value):
    high = lax.reduce_precision(value, 8, 7)
    return high.astype(jnp.bfloat16), (value - high).astype(jnp.bfloat16)


def local(amplitudes, integrals, eps_vir, eps_occ, panel_owner, block_target):
    me = lax.axis_index("vir")
    senders = lax.axis_size("vir")
    depth, col_count = integrals.shape
    blocks_dev = block_target.shape[0] // senders
    block = col_count // blocks_dev
    lanes = 128

    owners = block_target.reshape(senders, blocks_dev) // blocks_dev
    position = jnp.arange(blocks_dev, dtype=jnp.int32)
    goes = lax.dynamic_index_in_dim(owners, me, 0, keepdims=False)[None, :] == jnp.arange(senders)[:, None]
    first = jnp.min(jnp.where(goes, position[None, :], blocks_dev - 1), axis=1)
    second = jnp.max(jnp.where(goes, position[None, :], 0), axis=1)

    comes = owners == me
    sends = jnp.any(comes, axis=1)
    order = jnp.arange(senders, dtype=jnp.int32)
    rank = jnp.sum((sends[None, :] & (order[None, :] < order[:, None])).astype(jnp.int32), axis=1)
    pair_of = jnp.arange(senders // 2, dtype=jnp.int32)
    sender_of = jnp.sum(
        jnp.where(sends[None, :] & (rank[None, :] == pair_of[:, None]), order[None, :], 0), axis=1
    )
    lead = jnp.min(jnp.where(comes, position[None, :], blocks_dev), axis=1)
    place = 2 * rank[:, None] + (position[None, :] != lead[:, None]).astype(jnp.int32)
    wanted = me * blocks_dev + position
    found = block_target.reshape(1, senders, blocks_dev) == wanted[:, None, None]
    source = jnp.sum(jnp.where(found, place[None], 0), axis=(1, 2))

    turned = integrals.T.reshape(blocks_dev, block, depth)
    one, two = turned[first], turned[second]
    energies = eps_vir.reshape(blocks_dev, block)
    sent_eps = jnp.concatenate([energies[first], energies[second]], axis=1)
    sent_eps = jnp.pad(sent_eps, ((0, 0), (0, 8 * lanes - 2 * block))).reshape(senders, 8, lanes)
    packed = jnp.concatenate(
        [one[:, :, :lanes], two[:, :, :lanes], jnp.concatenate([one[:, :, lanes:], two[:, :, lanes:]], 2), sent_eps], 1
    )
    arrived = lax.all_to_all(packed, "vir", split_axis=0, concat_axis=0, tiled=True)

    panels = broadcast_panels(amplitudes, panel_owner, DIGITS)
    pieces = panels.reshape(N_OCC, depth, panels.shape[1])
    ordered = jnp.concatenate(
        [pieces[:, :lanes].reshape(-1, panels.shape[1]), pieces[:, lanes:].reshape(-1, panels.shape[1])], 0
    )
    high, low = split(ordered)

    compact = arrived[sender_of]
    rows = 3 * block
    ladder = ladder_of(compact[:, :rows], high, low)
    ladder = ladder.reshape(blocks_dev, block, ladder.shape[2])
    eps = compact[:, rows:].reshape(senders // 2, 8 * lanes)[:, : 2 * block].reshape(blocks_dev, block)
    scaled = ladder[source] / (eps[source][:, :, None] - eps_occ[None, None, :])
    return scaled.reshape(col_count, ladder.shape[2])


def solution(mesh):
    in_specs = (P("vir", "occ"), P("occ", "vir"), P("vir"), P("occ"), P(), P())
    out_specs = P("vir", "occ")
    return jax.shard_map(local, mesh=mesh, in_specs=in_specs, out_specs=out_specs, check_vma=False)
```

```python
import functools

import jax
import jax.numpy as jnp
from jax import lax
from jax.experimental import pallas as pl
from jax.experimental.pallas import tpu as pltpu
from jax.sharding import PartitionSpec as P

MESH = pl.DeviceIdType.MESH
STEPS = 12
N_OCC = 4
DIGITS = ((1, 2), (2, 4), (8, 2), (16, 4))


def remote(src, dst, sems, k, peer):
    send, recv = sems
    return pltpu.make_async_remote_copy(
        src_ref=src, dst_ref=dst, send_sem=send.at[k], recv_sem=recv.at[k], device_id=peer, device_id_type=MESH
    )


def gcd16(n):
    g = 16
    while n % g:
        g //= 2
    return g


def panel_kernel(digits, per_step, owner_ref, amp_ref, out_ref, *scratch):
    levels = len(digits)
    arrived, kept, sems = scratch[:levels], scratch[levels : 2 * levels - 1], scratch[2 * levels - 1 :]
    occ, vir = lax.axis_index("occ"), lax.axis_index("vir")
    mine = [(vir // stride) % size for stride, size in digits]

    def along(level, digit):
        stride, _ = digits[level]
        return (occ, vir + (digit - mine[level]) * stride)

    peers = []
    for level, (_, size) in enumerate(digits):
        peers += [along(level, lax.rem(mine[level] + d, size)) for d in range(1, size)]
    barrier = pltpu.get_barrier_semaphore()
    for peer in peers:
        pl.semaphore_signal(barrier, inc=1, device_id=peer, device_id_type=MESH)
    pl.semaphore_wait(barrier, len(peers))

    k = 0
    started = []
    current, base, bases, lengths = amp_ref, 0, [], []
    length = amp_ref.shape[0]
    for level, (stride, size) in enumerate(digits):
        part = length // size
        copies = []
        for d in range(1, size):
            digit = lax.rem(mine[level] + d, size)
            copies.append(
                remote(current.at[pl.ds(digit * part, part)], arrived[level].at[d - 1], sems, k, along(level, digit))
            )
            k += 1
        for copy in copies:
            copy.start()
        offset = mine[level] * part
        base = base + offset
        target, target_base = (kept[level], 0) if level < levels - 1 else (out_ref, base)
        for copy in copies:
            copy.wait_recv()
        group = min(gcd16(part), per_step)
        for g in range(part // group):
            holder = owner_ref[(base + g * group) // per_step]
            digit = (holder // stride) % size
            value = current[pl.ds(offset + g * group, group)]
            for d in range(1, size):
                source = lax.rem(mine[level] + size - d, size)
                value = jnp.where(digit == source, arrived[level][d - 1, pl.ds(g * group, group)], value)
            target[pl.ds(target_base + g * group, group)] = value
        started += copies
        current, length = (target, part)
        bases.append(base)
        lengths.append(part)

    for level in range(levels - 1, -1, -1):
        piece = out_ref.at[pl.ds(bases[level], lengths[level])]
        copies = []
        for d in range(1, digits[level][1]):
            digit = lax.rem(mine[level] + d, digits[level][1])
            copies.append(remote(piece, piece, sems, k, along(level, digit)))
            k += 1
        for copy in copies:
            copy.start()
        for copy in copies:
            copy.wait_recv()
        started += copies

    for copy in started:
        copy.wait_send()


def broadcast_panels(amplitudes, panel_owner, digits):
    rows, cols = amplitudes.shape
    units = (rows // 8) * (cols // 128)
    amps = amplitudes.reshape(rows // 8, 8, cols // 128, 128).transpose(0, 2, 1, 3).reshape(units, 8, 128)
    per_step = units // STEPS
    arrived, kept, length, count = [], [], units, 0
    for level, (_, size) in enumerate(digits):
        length //= size
        arrived.append(pltpu.VMEM((size - 1, length, 8, 128), jnp.float32))
        kept.append(pltpu.VMEM((length, 8, 128), jnp.float32))
        count += (size - 1) * 2
    out = pl.pallas_call(
        functools.partial(panel_kernel, digits, per_step),
        out_shape=jax.ShapeDtypeStruct((units, 8, 128), jnp.float32),
        in_specs=[pl.BlockSpec(memory_space=pltpu.SMEM), pl.BlockSpec(memory_space=pltpu.VMEM)],
        out_specs=pl.BlockSpec(memory_space=pltpu.VMEM),
        scratch_shapes=arrived
        + kept[:-1]
        + [
            pltpu.SemaphoreType.DMA((count,)),
            pltpu.SemaphoreType.DMA((count,)),
        ],
        compiler_params=pltpu.CompilerParams(collective_id=0, has_side_effects=True),
        name="panels",
    )(panel_owner, amps)
    return out.reshape(rows // 8, cols // 128, 8, 128).transpose(0, 2, 1, 3).reshape(rows, cols)


CHUNKS = 5
LANES = 128


def chunk_rows(block):
    size = 3 * (block // CHUNKS)
    sizes = [size + 8] + [size] * (CHUNKS - 1)
    return [sum(sizes[:c]) for c in range(CHUNKS)], sizes


def pack_kernel(first_ref, second_ref, ints_ref, eps_ref, out_ref, turned):
    depth, col_count = ints_ref.shape
    blocks = eps_ref.shape[0]
    block = col_count // blocks
    group = 8
    fine = block // CHUNKS
    offsets, _ = chunk_rows(block)

    @pl.when(pl.program_id(0) == 0)
    def _():
        for n in range(blocks // group):
            at = slice(n * group * block, (n + 1) * group * block)
            turned[at, 0:depth] = ints_ref[:, at].T

    low_lane = lax.broadcasted_iota(jnp.int32, (block, LANES), 1) < LANES // 2
    for i in range(out_ref.shape[0]):
        dest = pl.program_id(0) * out_ref.shape[0] + i
        one, two = first_ref[dest], second_ref[dest]
        row_one, row_two = pl.multiple_of(one * block, 8), pl.multiple_of(two * block, 8)
        main_one, main_two = turned[pl.ds(row_one, block), 0:LANES], turned[pl.ds(row_two, block), 0:LANES]
        fold = jnp.where(
            low_lane,
            turned[pl.ds(row_one, block), LANES : 2 * LANES],
            pltpu.roll(turned[pl.ds(row_two, block), LANES : 2 * LANES], LANES // 2, 1),
        )
        for c, offset in enumerate(offsets):
            part = slice(c * fine, (c + 1) * fine)
            out_ref[i, offset : offset + fine] = main_one[part]
            out_ref[i, offset + fine : offset + 2 * fine] = main_two[part]
            out_ref[i, offset + 2 * fine : offset + 3 * fine] = fold[part]
        spare = offsets[0] + 3 * fine
        out_ref[i, spare : spare + 1] = eps_ref[pl.ds(one, 1)]
        out_ref[i, spare + 1 : spare + 2] = eps_ref[pl.ds(two, 1)]
        out_ref[i, spare + 2 : spare + 8] = jnp.zeros((6, LANES), jnp.float32)


def pack(integrals, energies, first, second):
    dests = first.shape[0]
    depth, col_count = integrals.shape
    blocks = energies.shape[0]
    rows = 3 * (col_count // blocks) + 8
    step = 8
    return pl.pallas_call(
        pack_kernel,
        out_shape=jax.ShapeDtypeStruct((dests, rows, LANES), jnp.float32),
        grid_spec=pltpu.PrefetchScalarGridSpec(
            num_scalar_prefetch=2,
            grid=(dests // step,),
            in_specs=[
                pl.BlockSpec((depth, col_count), lambda i, *_: (0, 0)),
                pl.BlockSpec((blocks, LANES), lambda i, *_: (0, 0)),
            ],
            out_specs=pl.BlockSpec((step, rows, LANES), lambda i, *_: (i, 0, 0)),
            scratch_shapes=[pltpu.VMEM((col_count, 2 * LANES), jnp.float32)],
        ),
        name="pack",
    )(first, second, integrals, energies)


def place_kernel(source_ref, ladder_ref, eps_ref, occ_ref, out_ref):
    chunks, _, two_fine, _ = ladder_ref.shape
    fine = two_fine // 2
    block = chunks * fine
    for i in range(out_ref.shape[0] // block):
        source = source_ref[pl.program_id(0) * (out_ref.shape[0] // block) + i]
        pair, half = source // 2, source % 2
        columns = eps_ref[pair].T
        column = jnp.where(half == 0, columns[:, 0:1], columns[:, 1:2])
        for c in range(chunks):
            value = ladder_ref[c, pair, pl.ds(pl.multiple_of(half * fine, 8), fine)]
            out_ref[pl.ds(i * block + c * fine, fine)] = value / (column[c * fine : (c + 1) * fine] - occ_ref[...])


def place(ladder, eps, eps_occ, source):
    chunks, pairs, two_fine, width = ladder.shape
    block = chunks * two_fine // 2
    blocks = source.shape[0]
    step = 8
    return pl.pallas_call(
        place_kernel,
        out_shape=jax.ShapeDtypeStruct((blocks * block, width), jnp.float32),
        grid_spec=pltpu.PrefetchScalarGridSpec(
            num_scalar_prefetch=1,
            grid=(blocks // step,),
            in_specs=[
                pl.BlockSpec(ladder.shape, lambda i, *_: (0, 0, 0, 0)),
                pl.BlockSpec(eps.shape, lambda i, *_: (0, 0, 0)),
                pl.BlockSpec((1, width), lambda i, *_: (0, 0)),
            ],
            out_specs=pl.BlockSpec((step * block, width), lambda i, *_: (i, 0)),
        ),
        name="place",
    )(source, ladder, eps, eps_occ[None, :])


def ladder_kernel(geometry, slot_ref, packed_ref, panel_ref, out_ref, eps_ref, *scratch):
    inner, senders = geometry
    near, scratch = scratch[:CHUNKS], scratch[CHUNKS:]
    (away, compact, held, passing, result, passing_result, panels, passing_panels, high, low, left_high, left_low,
     xy_send, xy_recv, own_sem, flip_send, flip_recv, send, recv, panel_send, panel_recv) = scratch
    pairs, slabs = compact.shape[1], near[0].shape[0] // 2
    share = pairs // N_OCC
    part = share // 2
    rows = compact.shape[2]
    fine = rows // 3
    width = panel_ref.shape[1]
    depth = panel_ref.shape[0] // N_OCC
    offsets, sizes = chunk_rows(fine * CHUNKS)

    occ, vir = lax.axis_index("occ"), lax.axis_index("vir")
    level = (vir // inner) % 2
    plane = (vir // (2 * inner)) * inner + vir % inner
    above, below, far = (lax.rem(occ + n, N_OCC) for n in (1, N_OCC - 1, 2))
    up, down = (above, vir), (below, vir)
    other = vir + inner * (1 - 2 * level)
    inside = (occ, other)
    turn = 2 * level - 1
    across = (lax.rem(occ + N_OCC + turn, N_OCC), other)
    core = vir % 2
    sibling = (occ, vir + 1 - 2 * core)

    def member(q):
        return (occ, (q // inner) * (2 * inner) + level * inner + q % inner)

    barrier = pltpu.get_barrier_semaphore()

    def greet(n, _):
        pl.semaphore_signal(barrier, inc=1, device_id=member(lax.rem(plane + n, slabs)), device_id_type=MESH)
        return 0

    lax.fori_loop(1, slabs, greet, 0)
    for peer in (up, down, inside, across):
        pl.semaphore_signal(barrier, inc=1, device_id=peer, device_id_type=MESH)
    pl.semaphore_wait(barrier, slabs - 1 + 4)

    def make(src, dst, sems, at, peer):
        return pltpu.make_async_remote_copy(
            src_ref=src, dst_ref=dst, send_sem=sems[0].at[at], recv_sem=sems[1].at[at], device_id=peer,
            device_id_type=MESH,
        )

    def span(c):
        return pl.ds(offsets[c], sizes[c])

    def away_of(c):
        return away.at[c] if c == 0 else away.at[c, :, pl.ds(0, sizes[c])]

    half = panel_ref.shape[0] // 2
    quarter = half // 2
    start = pl.multiple_of(core * half, 8)

    def panel_rows(which, offset, size):
        return panels.at[which, pl.ds(start + offset, size)]

    panel_sems = (panel_send, panel_recv)
    own_rows = lambda offset, size: panel_ref.at[pl.ds(start + offset, size)]
    panel_copies = [
        make(own_rows(0, quarter), passing_panels.at[0], panel_sems, 0, up),
        make(own_rows(quarter, quarter), passing_panels.at[1], panel_sems, 1, down),
        make(own_rows(0, half), panel_rows(occ, 0, half), panel_sems, 2, up),
        make(own_rows(0, half), panel_rows(occ, 0, half), panel_sems, 3, down),
        make(passing_panels.at[0], panel_rows(below, 0, quarter), panel_sems, 4, up),
        make(passing_panels.at[1], panel_rows(above, quarter, quarter), panel_sems, 5, down),
        make(panel_rows(below, 0, half), panel_rows(below, 0, half), panel_sems, 6, sibling),
        make(panel_rows(above, 0, half), panel_rows(above, 0, half), panel_sems, 7, sibling),
        make(panel_rows(far, 0, half), panel_rows(far, 0, half), panel_sems, 8, sibling),
    ]
    own_panel = pltpu.make_async_copy(panel_ref, panels.at[occ], own_sem.at[0])
    own_panel.start()
    for k in range(4):
        panel_copies[k].start()

    def scatter(c):
        def one(n, _):
            q = lax.rem(plane + n, slabs)
            make(packed_ref.at[level, q, span(c)], near[c].at[plane], (xy_send, xy_recv), 2 * c, member(q)).start()
            make(packed_ref.at[1 - level, q, span(c)], away_of(c).at[plane], (xy_send, xy_recv), 2 * c + 1,
                 member(q)).start()
            return 0

        lax.fori_loop(1, slabs, one, 0)
        own_of(c, 0).start()
        own_of(c, 1).start()

    def own_of(c, which):
        if which == 0:
            return pltpu.make_async_copy(packed_ref.at[level, plane, span(c)], near[c].at[plane], own_sem.at[1 + 2 * c])
        return pltpu.make_async_copy(
            packed_ref.at[1 - level, plane, span(c)], away_of(c).at[plane], own_sem.at[2 + 2 * c]
        )

    def whole(ref, count, sem):
        at = ref.at[pl.ds(0, count)]
        return pltpu.make_async_copy(at, at, sem)

    def flips(c):
        count = slabs // 2
        source = away_of(c)
        return [
            make(source.at[pl.ds(n * count, count)], near[c].at[pl.ds(slabs + n * count, count)],
                 (flip_send, flip_recv), 2 * c + n, peer)
            for n, peer in enumerate((inside, across))
        ]

    def exchange(c, kind):
        sems, at = (send, recv), 12 * c + kind
        mine = pl.ds(occ * share, share)
        to = lambda which, offset=0, size=share: pl.ds(which * share + offset, size)
        if kind == 0:
            return make(compact.at[c, to(far, 0, part)], passing.at[c, 0], sems, at, up)
        if kind == 1:
            return make(compact.at[c, to(far, part, part)], passing.at[c, 1], sems, at, down)
        if kind == 2:
            return make(compact.at[c, to(above)], held.at[c, occ], sems, at, up)
        if kind == 3:
            return make(compact.at[c, to(below)], held.at[c, occ], sems, at, down)
        if kind == 4:
            return make(passing.at[c, 0], held.at[c, below, pl.ds(0, part)], sems, at, up)
        if kind == 5:
            return make(passing.at[c, 1], held.at[c, above, pl.ds(part, part)], sems, at, down)
        if kind == 6:
            return make(result.at[c, far, pl.ds(0, part)], passing_result.at[c, 0], sems, at, up)
        if kind == 7:
            return make(result.at[c, far, pl.ds(part, part)], passing_result.at[c, 1], sems, at, down)
        if kind == 8:
            return make(result.at[c, above], out_ref.at[c, mine], sems, at, up)
        if kind == 9:
            return make(result.at[c, below], out_ref.at[c, mine], sems, at, down)
        if kind == 10:
            return make(passing_result.at[c, 0], out_ref.at[c, to(below, 0, part)], sems, at, up)
        return make(passing_result.at[c, 1], out_ref.at[c, to(above, part, part)], sems, at, down)

    def gather(c):
        whole(away_of(c), slabs - 1, xy_recv.at[2 * c + 1]).wait()
        own_of(c, 1).wait()
        for copy in flips(c):
            copy.start()
        whole(near[c], slabs - 1, xy_recv.at[2 * c]).wait()
        own_of(c, 0).wait()

    def select(c):
        for copy in flips(c):
            copy.wait_recv()

        def one(p, _):
            slab = near[c][slot_ref[p]]
            compact[c, p] = slab[:rows]
            if c == 0:
                eps_ref[p] = slab[rows : rows + 8]
            return 0

        lax.fori_loop(0, pairs, one, 0)
        for kind in range(4):
            exchange(c, kind).start()
        local = pl.ds(occ * share, share)

        def keep(p, _):
            held[c, occ, p] = compact[c, occ * share + p]
            return 0

        lax.fori_loop(0, share, keep, 0)

    def relay(c):
        for n in range(2):
            exchange(c, n).wait_recv()
            exchange(c, 4 + n).start()

    def prepare():
        own_panel.wait()
        for n in range(N_OCC):
            pieces = ((n * depth, n * LANES, LANES), (n * depth + LANES, N_OCC * LANES + n * (depth - LANES), depth - LANES))
            for origin, target, count in pieces:
                for o in range(N_OCC):
                    value = panels[o, origin : origin + count]
                    upper = value.astype(jnp.bfloat16)
                    high[target : target + count, o * width : (o + 1) * width] = upper
                    low[target : target + count, o * width : (o + 1) * width] = (
                        value - upper.astype(jnp.float32)
                    ).astype(jnp.bfloat16)

    def compute(c):
        for kind in range(2, 6):
            exchange(c, kind).wait_recv()
        low_lane = lax.broadcasted_iota(jnp.int32, (fine, LANES), 1) < LANES // 2

        def arrange(p, _):
            turned = slot_ref[occ * share + p] >= slabs + slabs // 2
            value = [
                jnp.where(turned, held[c, lax.rem(n + N_OCC - turn, N_OCC), p], held[c, n, p]) for n in range(N_OCC)
            ]
            tiles = [v[: 2 * fine] for v in value]
            folds = [v[2 * fine :] for v in value]
            for n in range(0, N_OCC, 2):
                one = jnp.where(low_lane, folds[n], pltpu.roll(folds[n + 1], LANES // 2, 1))
                two = jnp.where(low_lane, pltpu.roll(folds[n], LANES // 2, 1), folds[n + 1])
                tiles.append(jnp.concatenate([one, two], axis=0))
            full = jnp.concatenate(tiles, axis=1)
            upper = full.astype(jnp.bfloat16)
            at = pl.ds(pl.multiple_of(p * 2 * fine, 16), 2 * fine)
            left_high[at] = upper
            left_low[at] = (full - upper.astype(jnp.float32)).astype(jnp.bfloat16)
            return 0

        lax.fori_loop(0, share, arrange, 0)
        for o in range(N_OCC):
            at = slice(o * width, (o + 1) * width)
            dot = lambda a, b: jnp.dot(a[...], b[:, at], preferred_element_type=jnp.float32)
            total = (dot(left_high, low) + dot(left_low, high)) + dot(left_high, high)
            result[c, o] = total.reshape(share, 2 * fine, width)
        out_ref[c, pl.ds(occ * share, share)] = result[c, occ]
        for kind in range(6, 10):
            exchange(c, kind).start()

    def relay_result(c):
        for n in range(2):
            exchange(c, 6 + n).wait_recv()
            exchange(c, 10 + n).start()

    scatter(0)
    scatter(1)
    for n in range(2):
        panel_copies[n].wait_recv()
        panel_copies[4 + n].start()
    for s in range(CHUNKS + 4):
        if 2 <= s + 2 < CHUNKS:
            scatter(s + 2)
        if s < CHUNKS:
            gather(s)
        if 0 <= s - 1 < CHUNKS:
            select(s - 1)
        if s == 1:
            for n in range(2):
                panel_copies[2 + n].wait_recv()
                panel_copies[6 + n].start()
            for n in range(2):
                panel_copies[4 + n].wait_recv()
            panel_copies[8].start()
        if 0 <= s - 2 < CHUNKS:
            relay(s - 2)
        if s == 2:
            for n in range(3):
                panel_copies[6 + n].wait_recv()
            prepare()
        if 0 <= s - 3 < CHUNKS:
            compute(s - 3)
        if 0 <= s - 4 < CHUNKS:
            relay_result(s - 4)

    for c in range(CHUNKS):
        for kind in range(8, 12):
            exchange(c, kind).wait_recv()
        for kind in range(12):
            exchange(c, kind).wait_send()
        for copy in flips(c):
            copy.wait_send()
        whole(near[c], slabs - 1, xy_send.at[2 * c]).wait()
        whole(away_of(c), slabs - 1, xy_send.at[2 * c + 1]).wait()
    for copy in panel_copies:
        copy.wait_send()


def ladder_of(packed, panel, slot_of, inner):
    _, slabs, total_rows, lanes = packed.shape
    pairs = slot_of.shape[0]
    depth, width = panel.shape
    share = pairs // N_OCC
    _, sizes = chunk_rows((total_rows - 8) // 3)
    rows = sizes[-1]
    fine = rows // 3
    f32, bf16 = jnp.float32, jnp.bfloat16
    vmem, dma = pl.BlockSpec(memory_space=pltpu.VMEM), pltpu.SemaphoreType.DMA
    return pl.pallas_call(
        functools.partial(ladder_kernel, (inner, 2 * slabs)),
        out_shape=[
            jax.ShapeDtypeStruct((CHUNKS, pairs, 2 * fine, width), f32),
            jax.ShapeDtypeStruct((pairs, 8, lanes), f32),
        ],
        in_specs=[pl.BlockSpec(memory_space=pltpu.SMEM), pl.BlockSpec(memory_space=pl.ANY), vmem],
        out_specs=[vmem, vmem],
        scratch_shapes=[pltpu.VMEM((2 * slabs, size, lanes), f32) for size in sizes]
        + [
            pltpu.VMEM((CHUNKS, slabs, sizes[0], lanes), f32),
            pltpu.VMEM((CHUNKS, pairs, rows, lanes), f32),
            pltpu.VMEM((CHUNKS, N_OCC, share, rows, lanes), f32),
            pltpu.VMEM((CHUNKS, 2, share // 2, rows, lanes), f32),
            pltpu.VMEM((CHUNKS, N_OCC, share, 2 * fine, width), f32),
            pltpu.VMEM((CHUNKS, 2, share // 2, 2 * fine, width), f32),
            pltpu.VMEM((N_OCC, depth, width), f32),
            pltpu.VMEM((2, depth // 4, width), f32),
            pltpu.VMEM((depth, N_OCC * width), bf16),
            pltpu.VMEM((depth, N_OCC * width), bf16),
            pltpu.VMEM((share * 2 * fine, depth), bf16),
            pltpu.VMEM((share * 2 * fine, depth), bf16),
            dma((2 * CHUNKS,)),
            dma((2 * CHUNKS,)),
            dma((1 + 2 * CHUNKS,)),
            dma((2 * CHUNKS,)),
            dma((2 * CHUNKS,)),
            dma((12 * CHUNKS,)),
            dma((12 * CHUNKS,)),
            dma((9,)),
            dma((9,)),
        ],
        compiler_params=pltpu.CompilerParams(collective_id=1, has_side_effects=True, vmem_limit_bytes=60 * 2**20),
        name="ladder",
    )(slot_of, packed, panel)


def local(amplitudes, integrals, eps_vir, eps_occ, panel_owner, block_target):
    me = lax.axis_index("vir")
    senders = lax.axis_size("vir")
    depth, col_count = integrals.shape
    blocks_dev = block_target.shape[0] // senders
    block = col_count // blocks_dev
    stride, levels = DIGITS[2]
    inner = stride
    slabs = senders // levels

    owners = block_target.reshape(senders, blocks_dev) // blocks_dev
    position = jnp.arange(blocks_dev, dtype=jnp.int32)
    order = jnp.arange(senders, dtype=jnp.int32)
    dest = order % slabs
    dest = (dest // inner) * (levels * inner) + (order // slabs) * inner + dest % inner
    goes = lax.dynamic_index_in_dim(owners, me, 0, keepdims=False)[None, :] == dest[:, None]
    first = jnp.min(jnp.where(goes, position[None, :], blocks_dev - 1), axis=1)
    second = jnp.max(jnp.where(goes, position[None, :], 0), axis=1)

    comes = owners == me
    sends = jnp.any(comes, axis=1)
    level = (order // inner) % levels
    slot = (order // (levels * inner)) * inner + order % inner
    slot = slot + jnp.where(level == (me // inner) % levels, 0, slabs)
    rank = jnp.sum((sends[None, :] & (slot[None, :] < slot[:, None])).astype(jnp.int32), axis=1)
    pair = jnp.arange(senders // 2, dtype=jnp.int32)
    slot_of = jnp.sum(jnp.where(sends[None, :] & (rank[None, :] == pair[:, None]), slot[None, :], 0), axis=1)
    lead = jnp.min(jnp.where(comes, position[None, :], blocks_dev), axis=1)
    stands = 2 * rank[:, None] + (position[None, :] != lead[:, None]).astype(jnp.int32)
    wanted = me * blocks_dev + position
    found = block_target.reshape(1, senders, blocks_dev) == wanted[:, None, None]
    source = jnp.sum(jnp.where(found, stands[None], 0), axis=(1, 2))

    energies = jnp.pad(eps_vir.reshape(blocks_dev, block), ((0, 0), (0, LANES - block)))
    packed = pack(integrals, energies, first, second)
    packed = packed.reshape(levels, slabs, packed.shape[1], LANES)
    panel = broadcast_panels(amplitudes, panel_owner, DIGITS)
    ladder, eps = ladder_of(packed, panel, slot_of, inner)
    return place(ladder, eps, eps_occ, source)


def solution(mesh):
    in_specs = (P("vir", "occ"), P("occ", "vir"), P("vir"), P("occ"), P(), P())
    out_specs = P("vir", "occ")
    return jax.shard_map(local, mesh=mesh, in_specs=in_specs, out_specs=out_specs, check_vma=False)
```

```python
import functools

import jax
import jax.numpy as jnp
from jax import lax
from jax.experimental import pallas as pl
from jax.experimental.pallas import tpu as pltpu
from jax.sharding import PartitionSpec as P

MESH = pl.DeviceIdType.MESH
STEPS = 12
N_OCC = 4
DIGITS = ((1, 2), (8, 2), (2, 4), (16, 4))


def gcd16(n):
    g = 16
    while n % g:
        g //= 2
    return g


CHUNKS = 5
LANES = 128


def chunk_rows(block):
    size = 3 * (block // CHUNKS)
    sizes = [size + 8] + [size] * (CHUNKS - 1)
    return [sum(sizes[:c]) for c in range(CHUNKS)], sizes


def pack_kernel(first_ref, second_ref, ints_ref, eps_ref, out_ref, turned):
    depth, col_count = ints_ref.shape
    blocks = eps_ref.shape[0]
    block = col_count // blocks
    group = 8
    fine = block // CHUNKS
    offsets, _ = chunk_rows(block)

    @pl.when(pl.program_id(0) == 0)
    def _():
        for n in range(blocks // group):
            at = slice(n * group * block, (n + 1) * group * block)
            turned[at, 0:depth] = ints_ref[:, at].T

    low_lane = lax.broadcasted_iota(jnp.int32, (block, LANES), 1) < LANES // 2
    for i in range(out_ref.shape[0]):
        dest = pl.program_id(0) * out_ref.shape[0] + i
        one, two = first_ref[dest], second_ref[dest]
        row_one, row_two = pl.multiple_of(one * block, 8), pl.multiple_of(two * block, 8)
        main_one, main_two = turned[pl.ds(row_one, block), 0:LANES], turned[pl.ds(row_two, block), 0:LANES]
        fold = jnp.where(
            low_lane,
            turned[pl.ds(row_one, block), LANES : 2 * LANES],
            pltpu.roll(turned[pl.ds(row_two, block), LANES : 2 * LANES], LANES // 2, 1),
        )
        for c, offset in enumerate(offsets):
            part = slice(c * fine, (c + 1) * fine)
            out_ref[i, offset : offset + fine] = main_one[part]
            out_ref[i, offset + fine : offset + 2 * fine] = main_two[part]
            out_ref[i, offset + 2 * fine : offset + 3 * fine] = fold[part]
        spare = offsets[0] + 3 * fine
        out_ref[i, spare : spare + 1] = eps_ref[pl.ds(one, 1)]
        out_ref[i, spare + 1 : spare + 2] = eps_ref[pl.ds(two, 1)]
        out_ref[i, spare + 2 : spare + 8] = jnp.zeros((6, LANES), jnp.float32)


def pack(integrals, energies, first, second):
    dests = first.shape[0]
    depth, col_count = integrals.shape
    blocks = energies.shape[0]
    rows = 3 * (col_count // blocks) + 8
    step = 8
    return pl.pallas_call(
        pack_kernel,
        out_shape=jax.ShapeDtypeStruct((dests, rows, LANES), jnp.float32),
        grid_spec=pltpu.PrefetchScalarGridSpec(
            num_scalar_prefetch=2,
            grid=(dests // step,),
            in_specs=[
                pl.BlockSpec((depth, col_count), lambda i, *_: (0, 0)),
                pl.BlockSpec((blocks, LANES), lambda i, *_: (0, 0)),
            ],
            out_specs=pl.BlockSpec((step, rows, LANES), lambda i, *_: (i, 0, 0)),
            scratch_shapes=[pltpu.VMEM((col_count, 2 * LANES), jnp.float32)],
        ),
        name="pack",
    )(first, second, integrals, energies)


def place_kernel(source_ref, ladder_ref, out_ref):
    chunks, _, two_fine, _ = ladder_ref.shape
    fine = two_fine // 2
    block = chunks * fine
    for i in range(out_ref.shape[0] // block):
        source = source_ref[pl.program_id(0) * (out_ref.shape[0] // block) + i]
        pair, half = source // 2, source % 2
        for c in range(chunks):
            out_ref[pl.ds(i * block + c * fine, fine)] = ladder_ref[c, pair, pl.ds(pl.multiple_of(half * fine, 8), fine)]


def place(ladder, source):
    chunks, pairs, two_fine, width = ladder.shape
    block = chunks * two_fine // 2
    blocks = source.shape[0]
    step = 8
    return pl.pallas_call(
        place_kernel,
        out_shape=jax.ShapeDtypeStruct((blocks * block, width), jnp.float32),
        grid_spec=pltpu.PrefetchScalarGridSpec(
            num_scalar_prefetch=1,
            grid=(blocks // step,),
            in_specs=[pl.BlockSpec(ladder.shape, lambda i, *_: (0, 0, 0, 0))],
            out_specs=pl.BlockSpec((step * block, width), lambda i, *_: (i, 0)),
        ),
        name="place",
    )(source, ladder)


def ladder_kernel(digits, slot_ref, owner_ref, packed_ref, amp_ref, eocc_ref, out_ref, *scratch):
    inner = digits[1][0]
    levels = len(digits)
    near, scratch = scratch[:CHUNKS], scratch[CHUNKS:]
    arrived, kept, scratch = scratch[:levels], scratch[levels : 2 * levels - 1], scratch[2 * levels - 1 :]
    (away, compact, held, passing, result, passing_result, panels, high, low, left_high, left_low, eps_ref, eps_col,
     energies, xy_send, xy_recv, own_sem, flip_send, flip_recv, send, recv, panel_send, panel_recv) = scratch
    pairs, slabs = compact.shape[1], near[0].shape[0] // 2
    share = pairs // N_OCC
    part = share // 2
    rows = compact.shape[2]
    fine = rows // 3
    width = out_ref.shape[3]
    units = amp_ref.shape[0]
    per_step, across_units = units // STEPS, width // LANES
    depth = (units // across_units) * 8 // N_OCC
    offsets, sizes = chunk_rows(fine * CHUNKS)

    occ, vir = lax.axis_index("occ"), lax.axis_index("vir")
    level = (vir // inner) % 2
    plane = (vir // (2 * inner)) * inner + vir % inner
    above, below, far = (lax.rem(occ + n, N_OCC) for n in (1, N_OCC - 1, 2))
    up, down = (above, vir), (below, vir)
    other = vir + inner * (1 - 2 * level)
    inside = (occ, other)
    turn = 2 * level - 1
    across = (lax.rem(occ + N_OCC + turn, N_OCC), other)
    core = vir % 2
    sibling = (occ, vir + 1 - 2 * core)

    def member(q):
        return (occ, (q // inner) * (2 * inner) + level * inner + q % inner)

    mine_digit = [(vir // stride) % size for stride, size in digits]

    def along(n, digit):
        return (occ, vir + (digit - mine_digit[n]) * digits[n][0])

    barrier = pltpu.get_barrier_semaphore()

    def greet(n, _):
        pl.semaphore_signal(barrier, inc=1, device_id=member(lax.rem(plane + n, slabs)), device_id_type=MESH)
        return 0

    lax.fori_loop(1, slabs, greet, 0)
    for peer in (up, down, inside, across):
        pl.semaphore_signal(barrier, inc=1, device_id=peer, device_id_type=MESH)
    pl.semaphore_wait(barrier, slabs - 1 + 4)

    def make(src, dst, sems, at, peer):
        return pltpu.make_async_remote_copy(
            src_ref=src, dst_ref=dst, send_sem=sems[0].at[at], recv_sem=sems[1].at[at], device_id=peer,
            device_id_type=MESH,
        )

    def span(c):
        return pl.ds(offsets[c], sizes[c])

    def away_of(c):
        return away.at[c] if c == 0 else away.at[c, :, pl.ds(0, sizes[c])]

    panel_sems = (panel_send, panel_recv)
    panel_copies = []

    def panel_start(pieces):
        copies = [make(src, dst, panel_sems, len(panel_copies) + n, peer) for n, (src, dst, peer) in enumerate(pieces)]
        panel_copies.extend(copies)
        for copy in copies:
            copy.start()
        return copies

    def panel_stages():
        current, base, length, bases, lengths = amp_ref, 0, units, [], []
        for n, (stride, size) in enumerate(digits):
            part = length // size
            pieces = []
            for d in range(1, size):
                digit = lax.rem(mine_digit[n] + d, size)
                pieces.append((current.at[pl.ds(digit * part, part)], arrived[n].at[d - 1], along(n, digit)))
            copies = panel_start(pieces)
            yield
            offset = mine_digit[n] * part
            base = base + offset
            target, target_base = (kept[n], 0) if n < levels - 1 else (panels.at[occ], base)
            for copy in copies:
                copy.wait_recv()
            group = min(gcd16(part), per_step)
            for g in range(part // group):
                holder = owner_ref[(base + g * group) // per_step]
                digit = (holder // stride) % size
                value = current[pl.ds(offset + g * group, group)]
                for d in range(1, size):
                    source = lax.rem(mine_digit[n] + size - d, size)
                    value = jnp.where(digit == source, arrived[n][d - 1, pl.ds(g * group, group)], value)
                target[pl.ds(target_base + g * group, group)] = value
            current, length = target, part
            bases.append(base)
            lengths.append(part)
        for n in range(levels - 1, 1, -1):
            piece = panels.at[occ, pl.ds(bases[n], lengths[n])]
            copies = panel_start(
                [(piece, piece, along(n, lax.rem(mine_digit[n] + d, digits[n][1]))) for d in range(1, digits[n][1])]
            )
            yield
            for copy in copies:
                copy.wait_recv()
        around = 2 * N_OCC
        z = 2 * occ + level
        z_up, z_down = (lax.rem(occ + level, N_OCC), other), (lax.rem(occ + N_OCC - 1 + level, N_OCC), other)
        quarter, half = lengths[1], lengths[0]
        core = vir % 2
        for n in range(1, around // 2 + 1):
            pieces = []
            for sign, peer in ((-1, z_up), (1, z_down))[: 2 if n < around // 2 else 1]:
                origin = lax.rem(z + around + sign * (n - 1), around)
                piece = panels.at[origin // 2, pl.ds(core * half + (origin % 2) * quarter, quarter)]
                pieces.append((piece, piece, peer))
            copies = panel_start(pieces)
            yield
            for copy in copies:
                copy.wait_recv()
        piece = panels.at[:, pl.ds(core * half, half)]
        copies = panel_start([(piece, piece, along(0, 1 - mine_digit[0]))])
        yield
        copies[0].wait_recv()
        prepare()
        yield

    energy_copies = [
        make(eocc_ref, energies.at[occ], (send, recv), 12 * CHUNKS, up),
        make(eocc_ref, energies.at[occ], (send, recv), 12 * CHUNKS + 1, down),
        make(energies.at[below], energies.at[below], (send, recv), 12 * CHUNKS + 2, up),
    ]

    def scatter(c):
        def one(n, _):
            q = lax.rem(plane + n, slabs)
            make(packed_ref.at[level, q, span(c)], near[c].at[plane], (xy_send, xy_recv), 2 * c, member(q)).start()
            make(packed_ref.at[1 - level, q, span(c)], away_of(c).at[plane], (xy_send, xy_recv), 2 * c + 1,
                 member(q)).start()
            return 0

        lax.fori_loop(1, slabs, one, 0)
        own_of(c, 0).start()
        own_of(c, 1).start()

    def own_of(c, which):
        if which == 0:
            return pltpu.make_async_copy(packed_ref.at[level, plane, span(c)], near[c].at[plane], own_sem.at[1 + 2 * c])
        return pltpu.make_async_copy(
            packed_ref.at[1 - level, plane, span(c)], away_of(c).at[plane], own_sem.at[2 + 2 * c]
        )

    def whole(ref, count, sem):
        at = ref.at[pl.ds(0, count)]
        return pltpu.make_async_copy(at, at, sem)

    def flips(c):
        count = slabs // 2
        source = away_of(c)
        return [
            make(source.at[pl.ds(n * count, count)], near[c].at[pl.ds(slabs + n * count, count)],
                 (flip_send, flip_recv), 2 * c + n, peer)
            for n, peer in enumerate((inside, across))
        ]

    def exchange(c, kind):
        sems, at = (send, recv), 12 * c + kind
        mine = pl.ds(occ * share, share)
        to = lambda which, offset=0, size=share: pl.ds(which * share + offset, size)
        if kind == 0:
            return make(compact.at[c, to(far, 0, part)], passing.at[c, 0], sems, at, up)
        if kind == 1:
            return make(compact.at[c, to(far, part, part)], passing.at[c, 1], sems, at, down)
        if kind == 2:
            return make(compact.at[c, to(above)], held.at[c, occ], sems, at, up)
        if kind == 3:
            return make(compact.at[c, to(below)], held.at[c, occ], sems, at, down)
        if kind == 4:
            return make(passing.at[c, 0], held.at[c, below, pl.ds(0, part)], sems, at, up)
        if kind == 5:
            return make(passing.at[c, 1], held.at[c, above, pl.ds(part, part)], sems, at, down)
        if kind == 6:
            return make(result.at[c, far, pl.ds(0, part)], passing_result.at[c, 0], sems, at, up)
        if kind == 7:
            return make(result.at[c, far, pl.ds(part, part)], passing_result.at[c, 1], sems, at, down)
        if kind == 8:
            return make(result.at[c, above], out_ref.at[c, mine], sems, at, up)
        if kind == 9:
            return make(result.at[c, below], out_ref.at[c, mine], sems, at, down)
        if kind == 10:
            return make(passing_result.at[c, 0], out_ref.at[c, to(below, 0, part)], sems, at, up)
        return make(passing_result.at[c, 1], out_ref.at[c, to(above, part, part)], sems, at, down)

    def gather(c):
        whole(away_of(c), slabs - 1, xy_recv.at[2 * c + 1]).wait()
        own_of(c, 1).wait()
        for copy in flips(c):
            copy.start()
        whole(near[c], slabs - 1, xy_recv.at[2 * c]).wait()
        own_of(c, 0).wait()

    def select(c):
        for copy in flips(c):
            copy.wait_recv()

        def one(p, _):
            slab = near[c][slot_ref[p]]
            compact[c, p] = slab[:rows]
            if c == 0:
                eps_ref[p] = slab[rows : rows + 8]
            return 0

        lax.fori_loop(0, pairs, one, 0)
        for kind in range(4):
            exchange(c, kind).start()
        local = pl.ds(occ * share, share)

        def keep(p, _):
            held[c, occ, p] = compact[c, occ * share + p]
            return 0

        lax.fori_loop(0, share, keep, 0)

    def relay(c):
        for n in range(2):
            exchange(c, n).wait_recv()
            exchange(c, 4 + n).start()

    def prepare():
        for n in range(N_OCC):
            pieces = ((n * depth, n * LANES, LANES), (n * depth + LANES, N_OCC * LANES + n * (depth - LANES), depth - LANES))
            for origin, target, count in pieces:
                for o in range(N_OCC):
                    stacked = panels[o, origin // 8 * across_units : (origin + count) // 8 * across_units]
                    stacked = stacked.reshape(count // 8, across_units, 8, LANES)
                    for k in range(across_units):
                        value = stacked[:, k].reshape(count, LANES)
                        upper = value.astype(jnp.bfloat16)
                        at = slice(o * width + k * LANES, o * width + (k + 1) * LANES)
                        high[target : target + count, at] = upper
                        low[target : target + count, at] = (value - upper.astype(jnp.float32)).astype(jnp.bfloat16)

    def compute(c):
        for kind in range(2, 6):
            exchange(c, kind).wait_recv()
        low_lane = lax.broadcasted_iota(jnp.int32, (fine, LANES), 1) < LANES // 2

        def arrange(p, _):
            turned = slot_ref[occ * share + p] >= slabs + slabs // 2
            value = [
                jnp.where(turned, held[c, lax.rem(n + N_OCC - turn, N_OCC), p], held[c, n, p]) for n in range(N_OCC)
            ]
            tiles = [v[: 2 * fine] for v in value]
            folds = [v[2 * fine :] for v in value]
            for n in range(0, N_OCC, 2):
                one = jnp.where(low_lane, folds[n], pltpu.roll(folds[n + 1], LANES // 2, 1))
                two = jnp.where(low_lane, pltpu.roll(folds[n], LANES // 2, 1), folds[n + 1])
                tiles.append(jnp.concatenate([one, two], axis=0))
            full = jnp.concatenate(tiles, axis=1)
            upper = full.astype(jnp.bfloat16)
            at = pl.ds(pl.multiple_of(p * 2 * fine, 16), 2 * fine)
            left_high[at] = upper
            left_low[at] = (full - upper.astype(jnp.float32)).astype(jnp.bfloat16)
            columns = eps_ref[occ * share + p].T[c * fine : (c + 1) * fine]
            eps_col[at] = jnp.concatenate([columns[:, 0:1], columns[:, 1:2]], axis=0)
            return 0

        lax.fori_loop(0, share, arrange, 0)
        for o in range(N_OCC):
            at = slice(o * width, (o + 1) * width)
            dot = lambda a, b: jnp.dot(a[...], b[:, at], preferred_element_type=jnp.float32)
            total = (dot(left_high, low) + dot(left_low, high)) + dot(left_high, high)
            total = total / (eps_col[...] - energies[o, 0:1])
            result[c, o] = total.reshape(share, 2 * fine, width)
        out_ref[c, pl.ds(occ * share, share)] = result[c, occ]
        for kind in range(6, 10):
            exchange(c, kind).start()

    def relay_result(c):
        for n in range(2):
            exchange(c, 6 + n).wait_recv()
            exchange(c, 10 + n).start()

    panel = panel_stages()
    next(panel, None)
    for n in range(2):
        energy_copies[n].start()
    energies[occ] = eocc_ref[...]
    scatter(0)
    for _ in range(3):
        next(panel, None)
    for s in range(CHUNKS + 4):
        if s < CHUNKS:
            gather(s)
        if s == 0:
            next(panel, None)
            next(panel, None)
        if 1 <= s + 1 < CHUNKS:
            scatter(s + 1)
        if 0 <= s - 1 < CHUNKS:
            select(s - 1)
        if s == 1:
            next(panel, None)
            for n in range(2):
                energy_copies[n].wait_recv()
            energy_copies[2].start()
        if s == 2:
            next(panel, None)
        if 0 <= s - 2 < CHUNKS:
            relay(s - 2)
        if s == 2:
            next(panel, None)
        if s == 3:
            for _ in range(3):
                next(panel, None)
            energy_copies[2].wait_recv()
        if 0 <= s - 3 < CHUNKS:
            compute(s - 3)
        if 0 <= s - 4 < CHUNKS:
            relay_result(s - 4)

    for c in range(CHUNKS):
        for kind in range(8, 12):
            exchange(c, kind).wait_recv()
        for kind in range(12):
            exchange(c, kind).wait_send()
        for copy in flips(c):
            copy.wait_send()
        whole(near[c], slabs - 1, xy_send.at[2 * c]).wait()
        whole(away_of(c), slabs - 1, xy_send.at[2 * c + 1]).wait()
    for copy in panel_copies + energy_copies:
        copy.wait_send()


def ladder_of(packed, amplitudes, eps_occ, panel_owner, slot_of, digits):
    _, slabs, total_rows, lanes = packed.shape
    pairs = slot_of.shape[0]
    panel_rows, width = amplitudes.shape
    share = pairs // N_OCC
    _, sizes = chunk_rows((total_rows - 8) // 3)
    rows = sizes[-1]
    fine = rows // 3
    f32, bf16 = jnp.float32, jnp.bfloat16
    vmem, dma = pl.BlockSpec(memory_space=pltpu.VMEM), pltpu.SemaphoreType.DMA
    smem = pl.BlockSpec(memory_space=pltpu.SMEM)
    units = (panel_rows // 8) * (width // lanes)
    amps = amplitudes.reshape(panel_rows // 8, 8, width // lanes, lanes).transpose(0, 2, 1, 3).reshape(units, 8, lanes)
    arrived, kept, length, count = [], [], units, 2 * N_OCC
    for n, (_, size) in enumerate(digits):
        length //= size
        arrived.append(pltpu.VMEM((size - 1, length, 8, lanes), f32))
        kept.append(pltpu.VMEM((length, 8, lanes), f32))
        count += (size - 1) * (2 if n > 1 else 1)
    return pl.pallas_call(
        functools.partial(ladder_kernel, digits),
        out_shape=jax.ShapeDtypeStruct((CHUNKS, pairs, 2 * fine, width), f32),
        in_specs=[smem, smem, pl.BlockSpec(memory_space=pl.ANY), vmem, vmem],
        out_specs=vmem,
        scratch_shapes=[pltpu.VMEM((2 * slabs, size, lanes), f32) for size in sizes]
        + arrived
        + kept[:-1]
        + [
            pltpu.VMEM((CHUNKS, slabs, sizes[0], lanes), f32),
            pltpu.VMEM((CHUNKS, pairs, rows, lanes), f32),
            pltpu.VMEM((CHUNKS, N_OCC, share, rows, lanes), f32),
            pltpu.VMEM((CHUNKS, 2, share // 2, rows, lanes), f32),
            pltpu.VMEM((CHUNKS, N_OCC, share, 2 * fine, width), f32),
            pltpu.VMEM((CHUNKS, 2, share // 2, 2 * fine, width), f32),
            pltpu.VMEM((N_OCC, units, 8, lanes), f32),
            pltpu.VMEM((panel_rows, N_OCC * width), bf16),
            pltpu.VMEM((panel_rows, N_OCC * width), bf16),
            pltpu.VMEM((share * 2 * fine, panel_rows), bf16),
            pltpu.VMEM((share * 2 * fine, panel_rows), bf16),
            pltpu.VMEM((pairs, 8, lanes), f32),
            pltpu.VMEM((share * 2 * fine, 1), f32),
            pltpu.VMEM((N_OCC, 8, width), f32),
            dma((2 * CHUNKS,)),
            dma((2 * CHUNKS,)),
            dma((1 + 2 * CHUNKS,)),
            dma((2 * CHUNKS,)),
            dma((2 * CHUNKS,)),
            dma((12 * CHUNKS + 3,)),
            dma((12 * CHUNKS + 3,)),
            dma((count,)),
            dma((count,)),
        ],
        compiler_params=pltpu.CompilerParams(collective_id=1, has_side_effects=True, vmem_limit_bytes=60 * 2**20),
        name="ladder",
    )(slot_of, panel_owner, packed, amps, jnp.broadcast_to(eps_occ[None, :], (8, width)))


def local(amplitudes, integrals, eps_vir, eps_occ, panel_owner, block_target):
    me = lax.axis_index("vir")
    senders = lax.axis_size("vir")
    depth, col_count = integrals.shape
    blocks_dev = block_target.shape[0] // senders
    block = col_count // blocks_dev
    stride, levels = DIGITS[1]
    inner = stride
    slabs = senders // levels

    owners = block_target.reshape(senders, blocks_dev) // blocks_dev
    position = jnp.arange(blocks_dev, dtype=jnp.int32)
    order = jnp.arange(senders, dtype=jnp.int32)
    dest = order % slabs
    dest = (dest // inner) * (levels * inner) + (order // slabs) * inner + dest % inner
    goes = lax.dynamic_index_in_dim(owners, me, 0, keepdims=False)[None, :] == dest[:, None]
    first = jnp.min(jnp.where(goes, position[None, :], blocks_dev - 1), axis=1)
    second = jnp.max(jnp.where(goes, position[None, :], 0), axis=1)

    comes = owners == me
    sends = jnp.any(comes, axis=1)
    level = (order // inner) % levels
    slot = (order // (levels * inner)) * inner + order % inner
    slot = slot + jnp.where(level == (me // inner) % levels, 0, slabs)
    rank = jnp.sum((sends[None, :] & (slot[None, :] < slot[:, None])).astype(jnp.int32), axis=1)
    pair = jnp.arange(senders // 2, dtype=jnp.int32)
    slot_of = jnp.sum(jnp.where(sends[None, :] & (rank[None, :] == pair[:, None]), slot[None, :], 0), axis=1)
    lead = jnp.min(jnp.where(comes, position[None, :], blocks_dev), axis=1)
    stands = 2 * rank[:, None] + (position[None, :] != lead[:, None]).astype(jnp.int32)
    wanted = me * blocks_dev + position
    found = block_target.reshape(1, senders, blocks_dev) == wanted[:, None, None]
    source = jnp.sum(jnp.where(found, stands[None], 0), axis=(1, 2))

    energies = jnp.pad(eps_vir.reshape(blocks_dev, block), ((0, 0), (0, LANES - block)))
    packed = pack(integrals, energies, first, second)
    packed = packed.reshape(levels, slabs, packed.shape[1], LANES)
    ladder = ladder_of(packed, amplitudes, eps_occ, panel_owner, slot_of, DIGITS)
    return place(ladder, source)


def solution(mesh):
    in_specs = (P("vir", "occ"), P("occ", "vir"), P("vir"), P("occ"), P(), P())
    out_specs = P("vir", "occ")
    return jax.shard_map(local, mesh=mesh, in_specs=in_specs, out_specs=out_specs, check_vma=False)
```

```python
import functools

import jax
import jax.numpy as jnp
from jax import lax
from jax.experimental import pallas as pl
from jax.experimental.pallas import tpu as pltpu
from jax.sharding import PartitionSpec as P

MESH = pl.DeviceIdType.MESH
STEPS = 12
N_OCC = 4
DIGITS = ((1, 2), (8, 2), (2, 4), (16, 4))


def gcd16(n):
    g = 16
    while n % g:
        g //= 2
    return g


CHUNKS = 10
LANES = 128
ORDER = (
    "A0", "P", "P", "A1", "B0", "P", "A2", "S0", "B1", "D0", "P", "A3", "S1", "R0", "P", "B2", "D1", "B3", "P",
    "R1", "S2", "S3", "A4", "A5", "P", "D2", "P", "B4", "R2", "P", "A6", "A7", "S4", "B5", "P", "D3", "A8",
    "S5", "R3", "B6", "R4", "B7", "P", "P", "B8", "D4", "R5", "S6", "C0", "S7", "A9", "Q0", "C1", "C2", "D5",
    "D6", "C3", "Q1", "S8", "B9", "D7", "Q2", "R6", "C4", "S9", "C5", "Q3", "R7", "R8", "D8", "R9", "Q4", "C6",
    "D9", "C7", "C8", "Q5", "C9", "Q6", "Q7", "Q8", "Q9",
)


def chunk_rows(block):
    size = 3 * (block // CHUNKS)
    sizes = [size + 8] + [size] * (CHUNKS - 1)
    return [sum(sizes[:c]) for c in range(CHUNKS)], sizes


def pack_kernel(first_ref, second_ref, ints_ref, eps_ref, out_ref, turned):
    depth, col_count = ints_ref.shape
    blocks = eps_ref.shape[0]
    block = col_count // blocks
    group = 8
    fine = block // CHUNKS
    offsets, _ = chunk_rows(block)

    @pl.when(pl.program_id(0) == 0)
    def _():
        for n in range(blocks // group):
            at = slice(n * group * block, (n + 1) * group * block)
            turned[at, 0:depth] = ints_ref[:, at].T

    low_lane = lax.broadcasted_iota(jnp.int32, (block, LANES), 1) < LANES // 2
    for i in range(out_ref.shape[0]):
        dest = pl.program_id(0) * out_ref.shape[0] + i
        one, two = first_ref[dest], second_ref[dest]
        row_one, row_two = pl.multiple_of(one * block, 8), pl.multiple_of(two * block, 8)
        main_one, main_two = turned[pl.ds(row_one, block), 0:LANES], turned[pl.ds(row_two, block), 0:LANES]
        fold = jnp.where(
            low_lane,
            turned[pl.ds(row_one, block), LANES : 2 * LANES],
            pltpu.roll(turned[pl.ds(row_two, block), LANES : 2 * LANES], LANES // 2, 1),
        )
        for c, offset in enumerate(offsets):
            part = slice(c * fine, (c + 1) * fine)
            out_ref[i, offset : offset + fine] = main_one[part]
            out_ref[i, offset + fine : offset + 2 * fine] = main_two[part]
            out_ref[i, offset + 2 * fine : offset + 3 * fine] = fold[part]
        spare = offsets[0] + 3 * fine
        out_ref[i, spare : spare + 1] = eps_ref[pl.ds(one, 1)]
        out_ref[i, spare + 1 : spare + 2] = eps_ref[pl.ds(two, 1)]
        out_ref[i, spare + 2 : spare + 8] = jnp.zeros((6, LANES), jnp.float32)


def pack(integrals, energies, first, second):
    dests = first.shape[0]
    depth, col_count = integrals.shape
    blocks = energies.shape[0]
    rows = 3 * (col_count // blocks) + 8
    step = 8
    return pl.pallas_call(
        pack_kernel,
        out_shape=jax.ShapeDtypeStruct((dests, rows, LANES), jnp.float32),
        grid_spec=pltpu.PrefetchScalarGridSpec(
            num_scalar_prefetch=2,
            grid=(dests // step,),
            in_specs=[
                pl.BlockSpec((depth, col_count), lambda i, *_: (0, 0)),
                pl.BlockSpec((blocks, LANES), lambda i, *_: (0, 0)),
            ],
            out_specs=pl.BlockSpec((step, rows, LANES), lambda i, *_: (i, 0, 0)),
            scratch_shapes=[pltpu.VMEM((col_count, 2 * LANES), jnp.float32)],
        ),
        name="pack",
    )(first, second, integrals, energies)


def place_kernel(source_ref, ladder_ref, out_ref):
    chunks, _, two_fine, _ = ladder_ref.shape
    fine = two_fine // 2
    block = chunks * fine
    for i in range(out_ref.shape[0] // block):
        source = source_ref[pl.program_id(0) * (out_ref.shape[0] // block) + i]
        pair, half = source // 2, source % 2
        for c in range(chunks):
            out_ref[pl.ds(i * block + c * fine, fine)] = ladder_ref[c, pair, pl.ds(pl.multiple_of(half * fine, 8), fine)]


def place(ladder, source):
    chunks, pairs, two_fine, width = ladder.shape
    block = chunks * two_fine // 2
    blocks = source.shape[0]
    step = 8
    return pl.pallas_call(
        place_kernel,
        out_shape=jax.ShapeDtypeStruct((blocks * block, width), jnp.float32),
        grid_spec=pltpu.PrefetchScalarGridSpec(
            num_scalar_prefetch=1,
            grid=(blocks // step,),
            in_specs=[pl.BlockSpec(ladder.shape, lambda i, *_: (0, 0, 0, 0))],
            out_specs=pl.BlockSpec((step * block, width), lambda i, *_: (i, 0)),
        ),
        name="place",
    )(source, ladder)


def ladder_kernel(digits, slot_ref, owner_ref, packed_ref, amp_ref, eocc_ref, out_ref, *scratch):
    inner = digits[1][0]
    levels = len(digits)
    near, scratch = scratch[:CHUNKS], scratch[CHUNKS:]
    arrived, kept, scratch = scratch[:levels], scratch[levels : 2 * levels - 1], scratch[2 * levels - 1 :]
    (away, compact, held, passing, result, passing_result, panels, high, low, left_high, left_low, eps_ref, eps_col,
     energies, xy_send, xy_recv, own_sem, flip_send, flip_recv, send, recv, panel_send, panel_recv) = scratch
    pairs, slabs = compact.shape[1], near[0].shape[0] // 2
    share = pairs // N_OCC
    part = share // 2
    rows = compact.shape[2]
    fine = rows // 3
    width = out_ref.shape[3]
    units = amp_ref.shape[0]
    per_step, across_units = units // STEPS, width // LANES
    depth = (units // across_units) * 8 // N_OCC
    offsets, sizes = chunk_rows(fine * CHUNKS)

    occ, vir = lax.axis_index("occ"), lax.axis_index("vir")
    level = (vir // inner) % 2
    plane = (vir // (2 * inner)) * inner + vir % inner
    above, below, far = (lax.rem(occ + n, N_OCC) for n in (1, N_OCC - 1, 2))
    up, down = (above, vir), (below, vir)
    other = vir + inner * (1 - 2 * level)
    inside = (occ, other)
    turn = 2 * level - 1
    across = (lax.rem(occ + N_OCC + turn, N_OCC), other)
    core = vir % 2
    sibling = (occ, vir + 1 - 2 * core)

    def member(q):
        return (occ, (q // inner) * (2 * inner) + level * inner + q % inner)

    mine_digit = [(vir // stride) % size for stride, size in digits]

    def along(n, digit):
        return (occ, vir + (digit - mine_digit[n]) * digits[n][0])

    barrier = pltpu.get_barrier_semaphore()

    def greet(n, _):
        pl.semaphore_signal(barrier, inc=1, device_id=member(lax.rem(plane + n, slabs)), device_id_type=MESH)
        return 0

    lax.fori_loop(1, slabs, greet, 0)
    for peer in (up, down, inside, across):
        pl.semaphore_signal(barrier, inc=1, device_id=peer, device_id_type=MESH)
    pl.semaphore_wait(barrier, slabs - 1 + 4)

    def make(src, dst, sems, at, peer):
        return pltpu.make_async_remote_copy(
            src_ref=src, dst_ref=dst, send_sem=sems[0].at[at], recv_sem=sems[1].at[at], device_id=peer,
            device_id_type=MESH,
        )

    def span(c):
        return pl.ds(offsets[c], sizes[c])

    def away_of(c):
        return away.at[c] if c == 0 else away.at[c, :, pl.ds(0, sizes[c])]

    panel_sems = (panel_send, panel_recv)
    panel_copies = []

    def panel_start(pieces):
        copies = [make(src, dst, panel_sems, len(panel_copies) + n, peer) for n, (src, dst, peer) in enumerate(pieces)]
        panel_copies.extend(copies)
        for copy in copies:
            copy.start()
        return copies

    def panel_stages():
        current, base, length, bases, lengths = amp_ref, 0, units, [], []
        for n, (stride, size) in enumerate(digits):
            part = length // size
            pieces = []
            for d in range(1, size):
                digit = lax.rem(mine_digit[n] + d, size)
                pieces.append((current.at[pl.ds(digit * part, part)], arrived[n].at[d - 1], along(n, digit)))
            copies = panel_start(pieces)
            yield
            offset = mine_digit[n] * part
            base = base + offset
            target, target_base = (kept[n], 0) if n < levels - 1 else (panels.at[occ], base)
            for copy in copies:
                copy.wait_recv()
            group = min(gcd16(part), per_step)
            for g in range(part // group):
                holder = owner_ref[(base + g * group) // per_step]
                digit = (holder // stride) % size
                value = current[pl.ds(offset + g * group, group)]
                for d in range(1, size):
                    source = lax.rem(mine_digit[n] + size - d, size)
                    value = jnp.where(digit == source, arrived[n][d - 1, pl.ds(g * group, group)], value)
                target[pl.ds(target_base + g * group, group)] = value
            current, length = target, part
            bases.append(base)
            lengths.append(part)
        for n in range(levels - 1, 1, -1):
            piece = panels.at[occ, pl.ds(bases[n], lengths[n])]
            copies = panel_start(
                [(piece, piece, along(n, lax.rem(mine_digit[n] + d, digits[n][1]))) for d in range(1, digits[n][1])]
            )
            yield
            for copy in copies:
                copy.wait_recv()
        around = 2 * N_OCC
        z = 2 * occ + level
        z_up, z_down = (lax.rem(occ + level, N_OCC), other), (lax.rem(occ + N_OCC - 1 + level, N_OCC), other)
        quarter, half = lengths[1], lengths[0]
        core = vir % 2
        for n in range(1, around // 2 + 1):
            pieces = []
            for sign, peer in ((-1, z_up), (1, z_down))[: 2 if n < around // 2 else 1]:
                origin = lax.rem(z + around + sign * (n - 1), around)
                piece = panels.at[origin // 2, pl.ds(core * half + (origin % 2) * quarter, quarter)]
                pieces.append((piece, piece, peer))
            copies = panel_start(pieces)
            yield
            for copy in copies:
                copy.wait_recv()
        piece = panels.at[:, pl.ds(core * half, half)]
        copies = panel_start([(piece, piece, along(0, 1 - mine_digit[0]))])
        yield
        copies[0].wait_recv()
        prepare()
        yield

    energy_copies = [
        make(eocc_ref, energies.at[occ], (send, recv), 12 * CHUNKS, up),
        make(eocc_ref, energies.at[occ], (send, recv), 12 * CHUNKS + 1, down),
        make(energies.at[below], energies.at[below], (send, recv), 12 * CHUNKS + 2, up),
    ]

    def scatter(c):
        def one(n, _):
            q = lax.rem(plane + n, slabs)
            make(packed_ref.at[level, q, span(c)], near[c].at[plane], (xy_send, xy_recv), 2 * c, member(q)).start()
            make(packed_ref.at[1 - level, q, span(c)], away_of(c).at[plane], (xy_send, xy_recv), 2 * c + 1,
                 member(q)).start()
            return 0

        lax.fori_loop(1, slabs, one, 0)
        own_of(c, 0).start()
        own_of(c, 1).start()

    def own_of(c, which):
        if which == 0:
            return pltpu.make_async_copy(packed_ref.at[level, plane, span(c)], near[c].at[plane], own_sem.at[1 + 2 * c])
        return pltpu.make_async_copy(
            packed_ref.at[1 - level, plane, span(c)], away_of(c).at[plane], own_sem.at[2 + 2 * c]
        )

    def whole(ref, count, sem):
        at = ref.at[pl.ds(0, count)]
        return pltpu.make_async_copy(at, at, sem)

    def flips(c):
        count = slabs // 2
        source = away_of(c)
        return [
            make(source.at[pl.ds(n * count, count)], near[c].at[pl.ds(slabs + n * count, count)],
                 (flip_send, flip_recv), 2 * c + n, peer)
            for n, peer in enumerate((inside, across))
        ]

    def exchange(c, kind):
        sems, at = (send, recv), 12 * c + kind
        mine = pl.ds(occ * share, share)
        to = lambda which, offset=0, size=share: pl.ds(which * share + offset, size)
        if kind == 0:
            return make(compact.at[c, to(far, 0, part)], passing.at[c, 0], sems, at, up)
        if kind == 1:
            return make(compact.at[c, to(far, part, part)], passing.at[c, 1], sems, at, down)
        if kind == 2:
            return make(compact.at[c, to(above)], held.at[c, occ], sems, at, up)
        if kind == 3:
            return make(compact.at[c, to(below)], held.at[c, occ], sems, at, down)
        if kind == 4:
            return make(passing.at[c, 0], held.at[c, below, pl.ds(0, part)], sems, at, up)
        if kind == 5:
            return make(passing.at[c, 1], held.at[c, above, pl.ds(part, part)], sems, at, down)
        if kind == 6:
            return make(result.at[c, far, pl.ds(0, part)], passing_result.at[c, 0], sems, at, up)
        if kind == 7:
            return make(result.at[c, far, pl.ds(part, part)], passing_result.at[c, 1], sems, at, down)
        if kind == 8:
            return make(result.at[c, above], out_ref.at[c, mine], sems, at, up)
        if kind == 9:
            return make(result.at[c, below], out_ref.at[c, mine], sems, at, down)
        if kind == 10:
            return make(passing_result.at[c, 0], out_ref.at[c, to(below, 0, part)], sems, at, up)
        return make(passing_result.at[c, 1], out_ref.at[c, to(above, part, part)], sems, at, down)

    def gather(c):
        whole(away_of(c), slabs - 1, xy_recv.at[2 * c + 1]).wait()
        own_of(c, 1).wait()
        for copy in flips(c):
            copy.start()
        whole(near[c], slabs - 1, xy_recv.at[2 * c]).wait()
        own_of(c, 0).wait()

    def select(c):
        for copy in flips(c):
            copy.wait_recv()

        def one(p, _):
            slab = near[c][slot_ref[p]]
            compact[c, p] = slab[:rows]
            if c == 0:
                eps_ref[p] = slab[rows : rows + 8]
            return 0

        lax.fori_loop(0, pairs, one, 0)
        for kind in range(2):
            exchange(c, kind).start()

    def direct(c):
        for kind in range(2, 4):
            exchange(c, kind).start()

        def keep(p, _):
            held[c, occ, p] = compact[c, occ * share + p]
            return 0

        lax.fori_loop(0, share, keep, 0)

    def relay(c):
        for n in range(2):
            exchange(c, n).wait_recv()
            exchange(c, 4 + n).start()

    def prepare():
        for n in range(N_OCC):
            pieces = ((n * depth, n * LANES, LANES), (n * depth + LANES, N_OCC * LANES + n * (depth - LANES), depth - LANES))
            for origin, target, count in pieces:
                for o in range(N_OCC):
                    stacked = panels[o, origin // 8 * across_units : (origin + count) // 8 * across_units]
                    stacked = stacked.reshape(count // 8, across_units, 8, LANES)
                    for k in range(across_units):
                        value = stacked[:, k].reshape(count, LANES)
                        upper = value.astype(jnp.bfloat16)
                        at = slice(o * width + k * LANES, o * width + (k + 1) * LANES)
                        high[target : target + count, at] = upper
                        low[target : target + count, at] = (value - upper.astype(jnp.float32)).astype(jnp.bfloat16)

    def compute(c):
        for kind in range(2, 6):
            exchange(c, kind).wait_recv()
        low_lane = lax.broadcasted_iota(jnp.int32, (fine, LANES), 1) < LANES // 2

        def arrange(p, _):
            turned = slot_ref[occ * share + p] >= slabs + slabs // 2
            value = [
                jnp.where(turned, held[c, lax.rem(n + N_OCC - turn, N_OCC), p], held[c, n, p]) for n in range(N_OCC)
            ]
            tiles = [v[: 2 * fine] for v in value]
            folds = [v[2 * fine :] for v in value]
            for n in range(0, N_OCC, 2):
                one = jnp.where(low_lane, folds[n], pltpu.roll(folds[n + 1], LANES // 2, 1))
                two = jnp.where(low_lane, pltpu.roll(folds[n], LANES // 2, 1), folds[n + 1])
                tiles.append(jnp.concatenate([one, two], axis=0))
            full = jnp.concatenate(tiles, axis=1)
            upper = full.astype(jnp.bfloat16)
            at = pl.ds(pl.multiple_of(p * 2 * fine, 16), 2 * fine)
            left_high[at] = upper
            left_low[at] = (full - upper.astype(jnp.float32)).astype(jnp.bfloat16)
            columns = eps_ref[occ * share + p].T[c * fine : (c + 1) * fine]
            eps_col[at] = jnp.concatenate([columns[:, 0:1], columns[:, 1:2]], axis=0)
            return 0

        lax.fori_loop(0, share, arrange, 0)
        for o in range(N_OCC):
            at = slice(o * width, (o + 1) * width)
            dot = lambda a, b: jnp.dot(a[...], b[:, at], preferred_element_type=jnp.float32)
            total = (dot(left_high, low) + dot(left_low, high)) + dot(left_high, high)
            total = total / (eps_col[...] - energies[o, 0:1])
            result[c, o] = total.reshape(share, 2 * fine, width)
        out_ref[c, pl.ds(occ * share, share)] = result[c, occ]
        for kind in range(6, 10):
            exchange(c, kind).start()

    def relay_result(c):
        for n in range(2):
            exchange(c, 6 + n).wait_recv()
            exchange(c, 10 + n).start()

    for n in range(2):
        energy_copies[n].start()
    energies[occ] = eocc_ref[...]
    panel = panel_stages()
    steps = {"A": scatter, "B": gather, "S": select, "D": direct, "R": relay, "C": compute, "Q": relay_result}
    for name in ORDER:
        if name == "P":
            next(panel, None)
            continue
        if name == "R0":
            for n in range(2):
                energy_copies[n].wait_recv()
            energy_copies[2].start()
        if name == "C0":
            energy_copies[2].wait_recv()
        steps[name[0]](int(name[1:]))

    for c in range(CHUNKS):
        for kind in range(8, 12):
            exchange(c, kind).wait_recv()
        for kind in range(12):
            exchange(c, kind).wait_send()
        for copy in flips(c):
            copy.wait_send()
        whole(near[c], slabs - 1, xy_send.at[2 * c]).wait()
        whole(away_of(c), slabs - 1, xy_send.at[2 * c + 1]).wait()
    for copy in panel_copies + energy_copies:
        copy.wait_send()


def ladder_of(packed, amplitudes, eps_occ, panel_owner, slot_of, digits):
    _, slabs, total_rows, lanes = packed.shape
    pairs = slot_of.shape[0]
    panel_rows, width = amplitudes.shape
    share = pairs // N_OCC
    _, sizes = chunk_rows((total_rows - 8) // 3)
    rows = sizes[-1]
    fine = rows // 3
    f32, bf16 = jnp.float32, jnp.bfloat16
    vmem, dma = pl.BlockSpec(memory_space=pltpu.VMEM), pltpu.SemaphoreType.DMA
    smem = pl.BlockSpec(memory_space=pltpu.SMEM)
    units = (panel_rows // 8) * (width // lanes)
    amps = amplitudes.reshape(panel_rows // 8, 8, width // lanes, lanes).transpose(0, 2, 1, 3).reshape(units, 8, lanes)
    arrived, kept, length, count = [], [], units, 2 * N_OCC
    for n, (_, size) in enumerate(digits):
        length //= size
        arrived.append(pltpu.VMEM((size - 1, length, 8, lanes), f32))
        kept.append(pltpu.VMEM((length, 8, lanes), f32))
        count += (size - 1) * (2 if n > 1 else 1)
    return pl.pallas_call(
        functools.partial(ladder_kernel, digits),
        out_shape=jax.ShapeDtypeStruct((CHUNKS, pairs, 2 * fine, width), f32),
        in_specs=[smem, smem, pl.BlockSpec(memory_space=pl.ANY), vmem, vmem],
        out_specs=vmem,
        scratch_shapes=[pltpu.VMEM((2 * slabs, size, lanes), f32) for size in sizes]
        + arrived
        + kept[:-1]
        + [
            pltpu.VMEM((CHUNKS, slabs, sizes[0], lanes), f32),
            pltpu.VMEM((CHUNKS, pairs, rows, lanes), f32),
            pltpu.VMEM((CHUNKS, N_OCC, share, rows, lanes), f32),
            pltpu.VMEM((CHUNKS, 2, share // 2, rows, lanes), f32),
            pltpu.VMEM((CHUNKS, N_OCC, share, 2 * fine, width), f32),
            pltpu.VMEM((CHUNKS, 2, share // 2, 2 * fine, width), f32),
            pltpu.VMEM((N_OCC, units, 8, lanes), f32),
            pltpu.VMEM((panel_rows, N_OCC * width), bf16),
            pltpu.VMEM((panel_rows, N_OCC * width), bf16),
            pltpu.VMEM((share * 2 * fine, panel_rows), bf16),
            pltpu.VMEM((share * 2 * fine, panel_rows), bf16),
            pltpu.VMEM((pairs, 8, lanes), f32),
            pltpu.VMEM((share * 2 * fine, 1), f32),
            pltpu.VMEM((N_OCC, 8, width), f32),
            dma((2 * CHUNKS,)),
            dma((2 * CHUNKS,)),
            dma((1 + 2 * CHUNKS,)),
            dma((2 * CHUNKS,)),
            dma((2 * CHUNKS,)),
            dma((12 * CHUNKS + 3,)),
            dma((12 * CHUNKS + 3,)),
            dma((count,)),
            dma((count,)),
        ],
        compiler_params=pltpu.CompilerParams(collective_id=1, has_side_effects=True, vmem_limit_bytes=60 * 2**20),
        name="ladder",
    )(slot_of, panel_owner, packed, amps, jnp.broadcast_to(eps_occ[None, :], (8, width)))


def local(amplitudes, integrals, eps_vir, eps_occ, panel_owner, block_target):
    me = lax.axis_index("vir")
    senders = lax.axis_size("vir")
    depth, col_count = integrals.shape
    blocks_dev = block_target.shape[0] // senders
    block = col_count // blocks_dev
    stride, levels = DIGITS[1]
    inner = stride
    slabs = senders // levels

    owners = block_target.reshape(senders, blocks_dev) // blocks_dev
    position = jnp.arange(blocks_dev, dtype=jnp.int32)
    order = jnp.arange(senders, dtype=jnp.int32)
    dest = order % slabs
    dest = (dest // inner) * (levels * inner) + (order // slabs) * inner + dest % inner
    goes = lax.dynamic_index_in_dim(owners, me, 0, keepdims=False)[None, :] == dest[:, None]
    first = jnp.min(jnp.where(goes, position[None, :], blocks_dev - 1), axis=1)
    second = jnp.max(jnp.where(goes, position[None, :], 0), axis=1)

    comes = owners == me
    sends = jnp.any(comes, axis=1)
    level = (order // inner) % levels
    slot = (order // (levels * inner)) * inner + order % inner
    slot = slot + jnp.where(level == (me // inner) % levels, 0, slabs)
    rank = jnp.sum((sends[None, :] & (slot[None, :] < slot[:, None])).astype(jnp.int32), axis=1)
    pair = jnp.arange(senders // 2, dtype=jnp.int32)
    slot_of = jnp.sum(jnp.where(sends[None, :] & (rank[None, :] == pair[:, None]), slot[None, :], 0), axis=1)
    lead = jnp.min(jnp.where(comes, position[None, :], blocks_dev), axis=1)
    stands = 2 * rank[:, None] + (position[None, :] != lead[:, None]).astype(jnp.int32)
    wanted = me * blocks_dev + position
    found = block_target.reshape(1, senders, blocks_dev) == wanted[:, None, None]
    source = jnp.sum(jnp.where(found, stands[None], 0), axis=(1, 2))

    energies = jnp.pad(eps_vir.reshape(blocks_dev, block), ((0, 0), (0, LANES - block)))
    packed = pack(integrals, energies, first, second)
    packed = packed.reshape(levels, slabs, packed.shape[1], LANES)
    ladder = ladder_of(packed, amplitudes, eps_occ, panel_owner, slot_of, DIGITS)
    return place(ladder, source)


def solution(mesh):
    in_specs = (P("vir", "occ"), P("occ", "vir"), P("vir"), P("occ"), P(), P())
    out_specs = P("vir", "occ")
    return jax.shard_map(local, mesh=mesh, in_specs=in_specs, out_specs=out_specs, check_vma=False)
```

```python
import functools

import jax
import jax.numpy as jnp
from jax import lax
from jax.experimental import pallas as pl
from jax.experimental.pallas import tpu as pltpu
from jax.sharding import PartitionSpec as P

MESH = pl.DeviceIdType.MESH
STEPS = 12
N_OCC = 4
DIGITS = ((1, 2), (8, 2), (2, 4), (16, 4))


def gcd16(n):
    g = 16
    while n % g:
        g //= 2
    return g


CHUNKS = 10
LANES = 128
ORDER = (
    "A0", "A1", "P", "B0", "A2", "P", "S0", "P", "B1", "R0", "B2", "P", "S1", "D0", "P", "P", "D1", "A3", "S2",
    "R1", "A4", "P", "A5", "B3", "B4", "A6", "S3", "S4", "P", "B5", "A7", "B6", "D2", "S5", "A8", "P", "S6",
    "B7", "R2", "R3", "P", "B8", "S7", "P", "D3", "R4", "P", "D4", "R5", "A9", "C0", "C1", "C2", "S8", "R6",
    "B9", "D5", "D6", "D7", "C3", "S9", "C4", "R7", "C5", "D8", "R8", "R9", "C6", "D9", "C7", "C8", "C9",
)


KINDS = 8


def chunk_rows(block):
    size = 3 * (block // CHUNKS)
    sizes = [size + 8] + [size] * (CHUNKS - 1)
    return [sum(sizes[:c]) for c in range(CHUNKS)], sizes


def pack_kernel(first_ref, second_ref, ints_ref, eps_ref, out_ref, turned):
    depth, col_count = ints_ref.shape
    blocks = eps_ref.shape[0]
    block = col_count // blocks
    group = 8
    fine = block // CHUNKS
    offsets, _ = chunk_rows(block)

    @pl.when(pl.program_id(0) == 0)
    def _():
        for n in range(blocks // group):
            at = slice(n * group * block, (n + 1) * group * block)
            turned[at, 0:depth] = ints_ref[:, at].T

    low_lane = lax.broadcasted_iota(jnp.int32, (block, LANES), 1) < LANES // 2
    for i in range(out_ref.shape[0]):
        dest = pl.program_id(0) * out_ref.shape[0] + i
        one, two = first_ref[dest], second_ref[dest]
        row_one, row_two = pl.multiple_of(one * block, 8), pl.multiple_of(two * block, 8)
        main_one, main_two = turned[pl.ds(row_one, block), 0:LANES], turned[pl.ds(row_two, block), 0:LANES]
        fold = jnp.where(
            low_lane,
            turned[pl.ds(row_one, block), LANES : 2 * LANES],
            pltpu.roll(turned[pl.ds(row_two, block), LANES : 2 * LANES], LANES // 2, 1),
        )
        for c, offset in enumerate(offsets):
            part = slice(c * fine, (c + 1) * fine)
            out_ref[i, offset : offset + fine] = main_one[part]
            out_ref[i, offset + fine : offset + 2 * fine] = main_two[part]
            out_ref[i, offset + 2 * fine : offset + 3 * fine] = fold[part]
        spare = offsets[0] + 3 * fine
        out_ref[i, spare : spare + 1] = eps_ref[pl.ds(one, 1)]
        out_ref[i, spare + 1 : spare + 2] = eps_ref[pl.ds(two, 1)]
        out_ref[i, spare + 2 : spare + 8] = jnp.zeros((6, LANES), jnp.float32)


def pack(integrals, energies, first, second):
    dests = first.shape[0]
    depth, col_count = integrals.shape
    blocks = energies.shape[0]
    rows = 3 * (col_count // blocks) + 8
    step = 8
    return pl.pallas_call(
        pack_kernel,
        out_shape=jax.ShapeDtypeStruct((dests, rows, LANES), jnp.float32),
        grid_spec=pltpu.PrefetchScalarGridSpec(
            num_scalar_prefetch=2,
            grid=(dests // step,),
            in_specs=[
                pl.BlockSpec((depth, col_count), lambda i, *_: (0, 0)),
                pl.BlockSpec((blocks, LANES), lambda i, *_: (0, 0)),
            ],
            out_specs=pl.BlockSpec((step, rows, LANES), lambda i, *_: (i, 0, 0)),
            scratch_shapes=[pltpu.VMEM((col_count, 2 * LANES), jnp.float32)],
        ),
        name="pack",
    )(first, second, integrals, energies)


def place_kernel(source_ref, ladder_ref, out_ref):
    chunks, _, two_fine, _ = ladder_ref.shape
    fine = two_fine // 2
    block = chunks * fine
    for i in range(out_ref.shape[0] // block):
        source = source_ref[pl.program_id(0) * (out_ref.shape[0] // block) + i]
        pair, half = source // 2, source % 2
        for c in range(chunks):
            out_ref[pl.ds(i * block + c * fine, fine)] = ladder_ref[c, pair, pl.ds(pl.multiple_of(half * fine, 8), fine)]


def place(ladder, source):
    chunks, pairs, two_fine, width = ladder.shape
    block = chunks * two_fine // 2
    blocks = source.shape[0]
    step = 8
    return pl.pallas_call(
        place_kernel,
        out_shape=jax.ShapeDtypeStruct((blocks * block, width), jnp.float32),
        grid_spec=pltpu.PrefetchScalarGridSpec(
            num_scalar_prefetch=1,
            grid=(blocks // step,),
            in_specs=[pl.BlockSpec(ladder.shape, lambda i, *_: (0, 0, 0, 0))],
            out_specs=pl.BlockSpec((step * block, width), lambda i, *_: (i, 0)),
        ),
        name="place",
    )(source, ladder)


def ladder_kernel(digits, slot_ref, owner_ref, packed_ref, amp_ref, eocc_ref, out_ref, *scratch):
    inner = digits[1][0]
    levels = len(digits)
    near, scratch = scratch[:CHUNKS], scratch[CHUNKS:]
    arrived, kept, scratch = scratch[:levels], scratch[levels : 2 * levels - 1], scratch[2 * levels - 1 :]
    (away, compact, held, result, panels, high, low, left_high, left_low, eps_ref, eps_col,
     energies, xy_send, xy_recv, own_sem, flip_send, flip_recv, send, recv, panel_send, panel_recv) = scratch
    pairs, slabs = compact.shape[1], near[0].shape[0] // 2
    share = pairs // N_OCC
    rows = compact.shape[2]
    fine = rows // 3
    width = out_ref.shape[3]
    units = amp_ref.shape[0]
    per_step, across_units = units // STEPS, width // LANES
    depth = (units // across_units) * 8 // N_OCC
    offsets, sizes = chunk_rows(fine * CHUNKS)

    occ, vir = lax.axis_index("occ"), lax.axis_index("vir")
    level = (vir // inner) % 2
    plane = (vir // (2 * inner)) * inner + vir % inner
    above, below, far = (lax.rem(occ + n, N_OCC) for n in (1, N_OCC - 1, 2))
    up, down = (above, vir), (below, vir)
    other = vir + inner * (1 - 2 * level)
    inside = (occ, other)
    turn = 2 * level - 1
    across = (lax.rem(occ + N_OCC + turn, N_OCC), other)
    core = vir % 2
    sibling = (occ, vir + 1 - 2 * core)

    def member(q):
        return (occ, (q // inner) * (2 * inner) + level * inner + q % inner)

    mine_digit = [(vir // stride) % size for stride, size in digits]

    def along(n, digit):
        return (occ, vir + (digit - mine_digit[n]) * digits[n][0])

    barrier = pltpu.get_barrier_semaphore()

    def greet(n, _):
        pl.semaphore_signal(barrier, inc=1, device_id=member(lax.rem(plane + n, slabs)), device_id_type=MESH)
        return 0

    lax.fori_loop(1, slabs, greet, 0)
    for peer in (up, down, inside, across):
        pl.semaphore_signal(barrier, inc=1, device_id=peer, device_id_type=MESH)
    pl.semaphore_wait(barrier, slabs - 1 + 4)

    def make(src, dst, sems, at, peer):
        return pltpu.make_async_remote_copy(
            src_ref=src, dst_ref=dst, send_sem=sems[0].at[at], recv_sem=sems[1].at[at], device_id=peer,
            device_id_type=MESH,
        )

    def span(c):
        return pl.ds(offsets[c], sizes[c])

    def away_of(c):
        return away.at[c] if c == 0 else away.at[c, :, pl.ds(0, sizes[c])]

    panel_sems = (panel_send, panel_recv)
    panel_copies = []

    def panel_start(pieces):
        copies = [make(src, dst, panel_sems, len(panel_copies) + n, peer) for n, (src, dst, peer) in enumerate(pieces)]
        panel_copies.extend(copies)
        for copy in copies:
            copy.start()
        return copies

    def panel_stages():
        current, base, length, bases, lengths = amp_ref, 0, units, [], []
        for n, (stride, size) in enumerate(digits):
            part = length // size
            pieces = []
            for d in range(1, size):
                digit = lax.rem(mine_digit[n] + d, size)
                pieces.append((current.at[pl.ds(digit * part, part)], arrived[n].at[d - 1], along(n, digit)))
            copies = panel_start(pieces)
            yield
            offset = mine_digit[n] * part
            base = base + offset
            target, target_base = (kept[n], 0) if n < levels - 1 else (panels.at[occ], base)
            for copy in copies:
                copy.wait_recv()
            group = min(gcd16(part), per_step)
            for g in range(part // group):
                holder = owner_ref[(base + g * group) // per_step]
                digit = (holder // stride) % size
                value = current[pl.ds(offset + g * group, group)]
                for d in range(1, size):
                    source = lax.rem(mine_digit[n] + size - d, size)
                    value = jnp.where(digit == source, arrived[n][d - 1, pl.ds(g * group, group)], value)
                target[pl.ds(target_base + g * group, group)] = value
            current, length = target, part
            bases.append(base)
            lengths.append(part)
        for n in range(levels - 1, 1, -1):
            piece = panels.at[occ, pl.ds(bases[n], lengths[n])]
            copies = panel_start(
                [(piece, piece, along(n, lax.rem(mine_digit[n] + d, digits[n][1]))) for d in range(1, digits[n][1])]
            )
            yield
            for copy in copies:
                copy.wait_recv()
        around = 2 * N_OCC
        z = 2 * occ + level
        z_up, z_down = (lax.rem(occ + level, N_OCC), other), (lax.rem(occ + N_OCC - 1 + level, N_OCC), other)
        quarter, half = lengths[1], lengths[0]
        core = vir % 2
        for n in range(1, around // 2 + 1):
            pieces = []
            for sign, peer in ((-1, z_up), (1, z_down))[: 2 if n < around // 2 else 1]:
                origin = lax.rem(z + around + sign * (n - 1), around)
                piece = panels.at[origin // 2, pl.ds(core * half + (origin % 2) * quarter, quarter)]
                pieces.append((piece, piece, peer))
            copies = panel_start(pieces)
            yield
            for copy in copies:
                copy.wait_recv()
        piece = panels.at[:, pl.ds(core * half, half)]
        copies = panel_start([(piece, piece, along(0, 1 - mine_digit[0]))])
        yield
        copies[0].wait_recv()
        prepare()
        yield

    energy_copies = [
        make(eocc_ref, energies.at[occ], (send, recv), KINDS * CHUNKS, up),
        make(eocc_ref, energies.at[occ], (send, recv), KINDS * CHUNKS + 1, down),
        make(energies.at[below], energies.at[below], (send, recv), KINDS * CHUNKS + 2, up),
    ]

    def scatter(c):
        def one(n, _):
            q = lax.rem(plane + n, slabs)
            make(packed_ref.at[level, q, span(c)], near[c].at[plane], (xy_send, xy_recv), 2 * c, member(q)).start()
            make(packed_ref.at[1 - level, q, span(c)], away_of(c).at[plane], (xy_send, xy_recv), 2 * c + 1,
                 member(q)).start()
            return 0

        lax.fori_loop(1, slabs, one, 0)
        own_of(c, 0).start()
        own_of(c, 1).start()

    def own_of(c, which):
        if which == 0:
            return pltpu.make_async_copy(packed_ref.at[level, plane, span(c)], near[c].at[plane], own_sem.at[1 + 2 * c])
        return pltpu.make_async_copy(
            packed_ref.at[1 - level, plane, span(c)], away_of(c).at[plane], own_sem.at[2 + 2 * c]
        )

    def whole(ref, count, sem):
        at = ref.at[pl.ds(0, count)]
        return pltpu.make_async_copy(at, at, sem)

    def flips(c):
        count = slabs // 2
        source = away_of(c)
        return [
            make(source.at[pl.ds(n * count, count)], near[c].at[pl.ds(slabs + n * count, count)],
                 (flip_send, flip_recv), 2 * c + n, peer)
            for n, peer in enumerate((inside, across))
        ]

    def exchange(c, kind):
        sems, at = (send, recv), KINDS * c + kind
        group = lambda shift: pl.ds(lax.rem(occ + N_OCC + shift, N_OCC) * share, share)
        if kind == 0:
            return make(compact.at[c, group(0)], held.at[c, 0, occ], sems, at, up)
        if kind == 1:
            return make(compact.at[c, group(1)], held.at[c, 1, occ], sems, at, down)
        if kind == 2:
            return make(compact.at[c, group(-1)], held.at[c, 1, occ], sems, at, up)
        if kind == 3:
            return make(compact.at[c, group(-2)], held.at[c, 0, occ], sems, at, down)
        if kind == 4:
            return make(held.at[c, 0, below], held.at[c, 1, below], sems, at, up)
        if kind == 5:
            return make(held.at[c, 1, above], held.at[c, 0, above], sems, at, down)
        if kind == 6:
            return make(result.at[c, 0], out_ref.at[c, group(-1)], sems, at, down)
        return make(result.at[c, 1], out_ref.at[c, group(-2)], sems, at, up)

    def gather(c):
        whole(away_of(c), slabs - 1, xy_recv.at[2 * c + 1]).wait()
        own_of(c, 1).wait()
        for copy in flips(c):
            copy.start()
        whole(near[c], slabs - 1, xy_recv.at[2 * c]).wait()
        own_of(c, 0).wait()

    def select(c):
        for copy in flips(c):
            copy.wait_recv()

        def one(p, _):
            slab = near[c][slot_ref[p]]
            compact[c, p] = slab[:rows]
            if c == 0:
                eps_ref[p] = slab[rows : rows + 8]
            return 0

        lax.fori_loop(0, pairs, one, 0)
        for kind in range(2):
            exchange(c, kind).start()

    def direct(c):
        for kind in range(2, 4):
            exchange(c, kind).start()

        def keep(p, _):
            for role in range(2):
                held[c, role, occ, p] = compact[c, lax.rem(occ + N_OCC - 1 - role, N_OCC) * share + p]
            return 0

        lax.fori_loop(0, share, keep, 0)

    def relay(c):
        for n in range(2):
            exchange(c, n).wait_recv()
            exchange(c, 4 + n).start()

    def prepare():
        for n in range(N_OCC):
            pieces = ((n * depth, n * LANES, LANES), (n * depth + LANES, N_OCC * LANES + n * (depth - LANES), depth - LANES))
            for origin, target, count in pieces:
                for o in range(N_OCC):
                    stacked = panels[o, origin // 8 * across_units : (origin + count) // 8 * across_units]
                    stacked = stacked.reshape(count // 8, across_units, 8, LANES)
                    for k in range(across_units):
                        value = stacked[:, k].reshape(count, LANES)
                        upper = value.astype(jnp.bfloat16)
                        at = slice(k * LANES, (k + 1) * LANES)
                        high[o, target : target + count, at] = upper
                        low[o, target : target + count, at] = (value - upper.astype(jnp.float32)).astype(jnp.bfloat16)

    def compute(c):
        for kind in range(2, 6):
            exchange(c, kind).wait_recv()
        low_lane = lax.broadcasted_iota(jnp.int32, (fine, LANES), 1) < LANES // 2

        def arrange(q, _):
            role, p = q // share, q % share
            number = lax.rem(occ + N_OCC - 1 - role, N_OCC) * share + p
            turned = slot_ref[number] >= slabs + slabs // 2
            value = [
                jnp.where(turned, held[c, role, lax.rem(n + N_OCC - turn, N_OCC), p], held[c, role, n, p])
                for n in range(N_OCC)
            ]
            tiles = [v[: 2 * fine] for v in value]
            folds = [v[2 * fine :] for v in value]
            for n in range(0, N_OCC, 2):
                one = jnp.where(low_lane, folds[n], pltpu.roll(folds[n + 1], LANES // 2, 1))
                two = jnp.where(low_lane, pltpu.roll(folds[n], LANES // 2, 1), folds[n + 1])
                tiles.append(jnp.concatenate([one, two], axis=0))
            full = jnp.concatenate(tiles, axis=1)
            upper = full.astype(jnp.bfloat16)
            at = pl.ds(pl.multiple_of(q * 2 * fine, 16), 2 * fine)
            left_high[at] = upper
            left_low[at] = (full - upper.astype(jnp.float32)).astype(jnp.bfloat16)
            columns = eps_ref[number].T[c * fine : (c + 1) * fine]
            eps_col[at] = jnp.concatenate([columns[:, 0:1], columns[:, 1:2]], axis=0)
            return 0

        lax.fori_loop(0, 2 * share, arrange, 0)
        tall = share * 2 * fine
        for role, other_one in enumerate((below, above)):
            rows_of = pl.ds(role * tall, tall)
            for o in (other_one, occ):
                dot = lambda a, b: jnp.dot(a[rows_of], b[o], preferred_element_type=jnp.float32)
                total = (dot(left_high, low) + dot(left_low, high)) + dot(left_high, high)
                total = total / (eps_col[rows_of] - energies[o, 0:1])
                total = total.reshape(share, 2 * fine, width)
                if o is occ:
                    out_ref[c, pl.ds(lax.rem(occ + N_OCC - 1 - role, N_OCC) * share, share)] = total
                else:
                    result[c, role] = total
        for kind in range(6, 8):
            exchange(c, kind).start()

    for n in range(2):
        energy_copies[n].start()
    energies[occ] = eocc_ref[...]
    panel = panel_stages()
    steps = {"A": scatter, "B": gather, "S": select, "D": direct, "R": relay, "C": compute}
    for name in ORDER:
        if name == "P":
            next(panel, None)
            continue
        if name == "R0":
            for n in range(2):
                energy_copies[n].wait_recv()
            energy_copies[2].start()
        if name == "C0":
            energy_copies[2].wait_recv()
        steps[name[0]](int(name[1:]))

    for c in range(CHUNKS):
        for kind in range(6, 8):
            exchange(c, kind).wait_recv()
        for kind in range(KINDS):
            exchange(c, kind).wait_send()
        for copy in flips(c):
            copy.wait_send()
        whole(near[c], slabs - 1, xy_send.at[2 * c]).wait()
        whole(away_of(c), slabs - 1, xy_send.at[2 * c + 1]).wait()
    for copy in panel_copies + energy_copies:
        copy.wait_send()


def ladder_of(packed, amplitudes, eps_occ, panel_owner, slot_of, digits):
    _, slabs, total_rows, lanes = packed.shape
    pairs = slot_of.shape[0]
    panel_rows, width = amplitudes.shape
    share = pairs // N_OCC
    _, sizes = chunk_rows((total_rows - 8) // 3)
    rows = sizes[-1]
    fine = rows // 3
    f32, bf16 = jnp.float32, jnp.bfloat16
    vmem, dma = pl.BlockSpec(memory_space=pltpu.VMEM), pltpu.SemaphoreType.DMA
    smem = pl.BlockSpec(memory_space=pltpu.SMEM)
    units = (panel_rows // 8) * (width // lanes)
    amps = amplitudes.reshape(panel_rows // 8, 8, width // lanes, lanes).transpose(0, 2, 1, 3).reshape(units, 8, lanes)
    arrived, kept, length, count = [], [], units, 2 * N_OCC
    for n, (_, size) in enumerate(digits):
        length //= size
        arrived.append(pltpu.VMEM((size - 1, length, 8, lanes), f32))
        kept.append(pltpu.VMEM((length, 8, lanes), f32))
        count += (size - 1) * (2 if n > 1 else 1)
    return pl.pallas_call(
        functools.partial(ladder_kernel, digits),
        out_shape=jax.ShapeDtypeStruct((CHUNKS, pairs, 2 * fine, width), f32),
        in_specs=[smem, smem, pl.BlockSpec(memory_space=pl.ANY), vmem, vmem],
        out_specs=vmem,
        scratch_shapes=[pltpu.VMEM((2 * slabs, size, lanes), f32) for size in sizes]
        + arrived
        + kept[:-1]
        + [
            pltpu.VMEM((CHUNKS, slabs, sizes[0], lanes), f32),
            pltpu.VMEM((CHUNKS, pairs, rows, lanes), f32),
            pltpu.VMEM((CHUNKS, 2, N_OCC, share, rows, lanes), f32),
            pltpu.VMEM((CHUNKS, 2, share, 2 * fine, width), f32),
            pltpu.VMEM((N_OCC, units, 8, lanes), f32),
            pltpu.VMEM((N_OCC, panel_rows, width), bf16),
            pltpu.VMEM((N_OCC, panel_rows, width), bf16),
            pltpu.VMEM((share * 4 * fine, panel_rows), bf16),
            pltpu.VMEM((share * 4 * fine, panel_rows), bf16),
            pltpu.VMEM((pairs, 8, lanes), f32),
            pltpu.VMEM((share * 4 * fine, 1), f32),
            pltpu.VMEM((N_OCC, 1, width), f32),
            dma((2 * CHUNKS,)),
            dma((2 * CHUNKS,)),
            dma((1 + 2 * CHUNKS,)),
            dma((2 * CHUNKS,)),
            dma((2 * CHUNKS,)),
            dma((KINDS * CHUNKS + 3,)),
            dma((KINDS * CHUNKS + 3,)),
            dma((count,)),
            dma((count,)),
        ],
        compiler_params=pltpu.CompilerParams(collective_id=1, has_side_effects=True, vmem_limit_bytes=60 * 2**20),
        name="ladder",
    )(slot_of, panel_owner, packed, amps, eps_occ[None, :])


def local(amplitudes, integrals, eps_vir, eps_occ, panel_owner, block_target):
    me = lax.axis_index("vir")
    senders = lax.axis_size("vir")
    depth, col_count = integrals.shape
    blocks_dev = block_target.shape[0] // senders
    block = col_count // blocks_dev
    stride, levels = DIGITS[1]
    inner = stride
    slabs = senders // levels

    owners = block_target.reshape(senders, blocks_dev) // blocks_dev
    position = jnp.arange(blocks_dev, dtype=jnp.int32)
    order = jnp.arange(senders, dtype=jnp.int32)
    dest = order % slabs
    dest = (dest // inner) * (levels * inner) + (order // slabs) * inner + dest % inner
    goes = lax.dynamic_index_in_dim(owners, me, 0, keepdims=False)[None, :] == dest[:, None]
    first = jnp.min(jnp.where(goes, position[None, :], blocks_dev - 1), axis=1)
    second = jnp.max(jnp.where(goes, position[None, :], 0), axis=1)

    comes = owners == me
    sends = jnp.any(comes, axis=1)
    level = (order // inner) % levels
    slot = (order // (levels * inner)) * inner + order % inner
    slot = slot + jnp.where(level == (me // inner) % levels, 0, slabs)
    rank = jnp.sum((sends[None, :] & (slot[None, :] < slot[:, None])).astype(jnp.int32), axis=1)
    pair = jnp.arange(senders // 2, dtype=jnp.int32)
    slot_of = jnp.sum(jnp.where(sends[None, :] & (rank[None, :] == pair[:, None]), slot[None, :], 0), axis=1)
    lead = jnp.min(jnp.where(comes, position[None, :], blocks_dev), axis=1)
    stands = 2 * rank[:, None] + (position[None, :] != lead[:, None]).astype(jnp.int32)
    wanted = me * blocks_dev + position
    found = block_target.reshape(1, senders, blocks_dev) == wanted[:, None, None]
    source = jnp.sum(jnp.where(found, stands[None], 0), axis=(1, 2))

    energies = jnp.pad(eps_vir.reshape(blocks_dev, block), ((0, 0), (0, LANES - block)))
    packed = pack(integrals, energies, first, second)
    packed = packed.reshape(levels, slabs, packed.shape[1], LANES)
    ladder = ladder_of(packed, amplitudes, eps_occ, panel_owner, slot_of, DIGITS)
    return place(ladder, source)


def solution(mesh):
    in_specs = (P("vir", "occ"), P("occ", "vir"), P("vir"), P("occ"), P(), P())
    out_specs = P("vir", "occ")
    return jax.shard_map(local, mesh=mesh, in_specs=in_specs, out_specs=out_specs, check_vma=False)
```

```python
import functools

import jax
import jax.numpy as jnp
from jax import lax
from jax.experimental import pallas as pl
from jax.experimental.pallas import tpu as pltpu
from jax.sharding import PartitionSpec as P

MESH = pl.DeviceIdType.MESH
STEPS = 12
N_OCC = 4
DIGITS = ((1, 2), (8, 2), (2, 4), (16, 4))


def gcd16(n):
    g = 16
    while n % g:
        g //= 2
    return g


CHUNKS = 10
LANES = 128
ORDER = (
    "A0", "A1", "P", "B0", "A2", "P", "S0", "P", "B1", "R0", "B2", "P", "S1", "D0", "P", "P", "D1", "A3", "S2",
    "R1", "A4", "P", "A5", "B3", "B4", "A6", "S3", "S4", "P", "B5", "A7", "B6", "D2", "S5", "A8", "P", "S6",
    "B7", "R2", "R3", "P", "B8", "S7", "P", "D3", "R4", "P", "D4", "R5", "A9", "C0", "C1", "C2", "S8", "R6",
    "B9", "D5", "D6", "D7", "C3", "S9", "C4", "R7", "C5", "D8", "R8", "R9", "C6", "D9", "C7", "C8", "C9",
)


KINDS = 8


def chunk_rows(block):
    size = 3 * (block // CHUNKS)
    return [size + 8] + [size] * (CHUNKS - 1)


def place_kernel(source_ref, ladder_ref, out_ref):
    chunks, _, two_fine, _ = ladder_ref.shape
    fine = two_fine // 2
    block = chunks * fine
    for i in range(out_ref.shape[0] // block):
        source = source_ref[pl.program_id(0) * (out_ref.shape[0] // block) + i]
        pair, half = source // 2, source % 2
        for c in range(chunks):
            out_ref[pl.ds(i * block + c * fine, fine)] = ladder_ref[c, pair, pl.ds(pl.multiple_of(half * fine, 8), fine)]


def place(ladder, source):
    chunks, pairs, two_fine, width = ladder.shape
    block = chunks * two_fine // 2
    blocks = source.shape[0]
    step = 8
    return pl.pallas_call(
        place_kernel,
        out_shape=jax.ShapeDtypeStruct((blocks * block, width), jnp.float32),
        grid_spec=pltpu.PrefetchScalarGridSpec(
            num_scalar_prefetch=1,
            grid=(blocks // step,),
            in_specs=[pl.BlockSpec(ladder.shape, lambda i, *_: (0, 0, 0, 0))],
            out_specs=pl.BlockSpec((step * block, width), lambda i, *_: (i, 0)),
        ),
        name="place",
    )(source, ladder)


def ladder_kernel(
    digits, slot_ref, owner_ref, first_ref, second_ref, ints_ref, evir_ref, amp_ref, eocc_ref, out_ref, *scratch
):
    inner = digits[1][0]
    levels = len(digits)
    near, away, packed, scratch = (
        scratch[:CHUNKS], scratch[CHUNKS : 2 * CHUNKS], scratch[2 * CHUNKS : 3 * CHUNKS], scratch[3 * CHUNKS :]
    )
    arrived, kept, scratch = scratch[:levels], scratch[levels : 2 * levels - 1], scratch[2 * levels - 1 :]
    (turned, compact, held, result, panels, high, low, left_high, left_low, eps_ref, eps_col,
     energies, xy_send, xy_recv, own_sem, flip_send, flip_recv, send, recv, panel_send, panel_recv) = scratch
    pairs, slabs = compact.shape[1], near[0].shape[0] // 2
    share = pairs // N_OCC
    rows = compact.shape[2]
    fine = rows // 3
    width = out_ref.shape[3]
    units = amp_ref.shape[0]
    per_step, across_units = units // STEPS, width // LANES
    depth = (units // across_units) * 8 // N_OCC
    block = fine * CHUNKS

    occ, vir = lax.axis_index("occ"), lax.axis_index("vir")
    level = (vir // inner) % 2
    plane = (vir // (2 * inner)) * inner + vir % inner
    above, below, far = (lax.rem(occ + n, N_OCC) for n in (1, N_OCC - 1, 2))
    up, down = (above, vir), (below, vir)
    other = vir + inner * (1 - 2 * level)
    inside = (occ, other)
    turn = 2 * level - 1
    across = (lax.rem(occ + N_OCC + turn, N_OCC), other)
    core = vir % 2
    sibling = (occ, vir + 1 - 2 * core)

    def member(q):
        return (occ, (q // inner) * (2 * inner) + level * inner + q % inner)

    mine_digit = [(vir // stride) % size for stride, size in digits]

    def along(n, digit):
        return (occ, vir + (digit - mine_digit[n]) * digits[n][0])

    barrier = pltpu.get_barrier_semaphore()

    def greet(n, _):
        pl.semaphore_signal(barrier, inc=1, device_id=member(lax.rem(plane + n, slabs)), device_id_type=MESH)
        return 0

    lax.fori_loop(1, slabs, greet, 0)
    for peer in (up, down, inside, across):
        pl.semaphore_signal(barrier, inc=1, device_id=peer, device_id_type=MESH)

    def make(src, dst, sems, at, peer):
        return pltpu.make_async_remote_copy(
            src_ref=src, dst_ref=dst, send_sem=sems[0].at[at], recv_sem=sems[1].at[at], device_id=peer,
            device_id_type=MESH,
        )

    def turn_over():
        span = 8 * block
        for n in range(ints_ref.shape[1] // span):
            at = slice(n * span, (n + 1) * span)
            turned[n * block : (n + 1) * block, :, 0 : ints_ref.shape[0]] = ints_ref[:, at].T.reshape(block, 8, ints_ref.shape[0])

    def pack(c):
        low_lane = lax.broadcasted_iota(jnp.int32, (fine, LANES), 1) < LANES // 2

        def one_owner(w, _):
            one, two = first_ref[w], second_ref[w]
            left, right = turned[one * CHUNKS + c], turned[two * CHUNKS + c]
            packed[c][w, 0:fine] = left[:, 0:LANES]
            packed[c][w, fine : 2 * fine] = right[:, 0:LANES]
            packed[c][w, 2 * fine : rows] = jnp.where(
                low_lane, left[:, LANES : 2 * LANES], pltpu.roll(right[:, LANES : 2 * LANES], LANES // 2, 1)
            )
            if c == 0:
                packed[c][w, rows : rows + 1] = evir_ref[one]
                packed[c][w, rows + 1 : rows + 2] = evir_ref[two]
                packed[c][w, rows + 2 : rows + 8] = jnp.zeros((6, LANES), jnp.float32)
            return 0

        lax.fori_loop(0, 2 * slabs, one_owner, 0)

    turn_over()
    pack(0)
    pl.semaphore_wait(barrier, slabs - 1 + 4)

    panel_sems = (panel_send, panel_recv)
    panel_copies = []

    def panel_start(pieces):
        copies = [make(src, dst, panel_sems, len(panel_copies) + n, peer) for n, (src, dst, peer) in enumerate(pieces)]
        panel_copies.extend(copies)
        for copy in copies:
            copy.start()
        return copies

    def panel_stages():
        current, base, length, bases, lengths = amp_ref, 0, units, [], []
        for n, (stride, size) in enumerate(digits):
            part = length // size
            pieces = []
            for d in range(1, size):
                digit = lax.rem(mine_digit[n] + d, size)
                pieces.append((current.at[pl.ds(digit * part, part)], arrived[n].at[d - 1], along(n, digit)))
            copies = panel_start(pieces)
            yield
            offset = mine_digit[n] * part
            base = base + offset
            target, target_base = (kept[n], 0) if n < levels - 1 else (panels.at[occ], base)
            for copy in copies:
                copy.wait_recv()
            group = min(gcd16(part), per_step)
            for g in range(part // group):
                holder = owner_ref[(base + g * group) // per_step]
                digit = (holder // stride) % size
                value = current[pl.ds(offset + g * group, group)]
                for d in range(1, size):
                    source = lax.rem(mine_digit[n] + size - d, size)
                    value = jnp.where(digit == source, arrived[n][d - 1, pl.ds(g * group, group)], value)
                target[pl.ds(target_base + g * group, group)] = value
            current, length = target, part
            bases.append(base)
            lengths.append(part)
        for n in range(levels - 1, 1, -1):
            piece = panels.at[occ, pl.ds(bases[n], lengths[n])]
            copies = panel_start(
                [(piece, piece, along(n, lax.rem(mine_digit[n] + d, digits[n][1]))) for d in range(1, digits[n][1])]
            )
            yield
            for copy in copies:
                copy.wait_recv()
        around = 2 * N_OCC
        z = 2 * occ + level
        z_up, z_down = (lax.rem(occ + level, N_OCC), other), (lax.rem(occ + N_OCC - 1 + level, N_OCC), other)
        quarter, half = lengths[1], lengths[0]
        core = vir % 2
        for n in range(1, around // 2 + 1):
            pieces = []
            for sign, peer in ((-1, z_up), (1, z_down))[: 2 if n < around // 2 else 1]:
                origin = lax.rem(z + around + sign * (n - 1), around)
                piece = panels.at[origin // 2, pl.ds(core * half + (origin % 2) * quarter, quarter)]
                pieces.append((piece, piece, peer))
            copies = panel_start(pieces)
            yield
            for copy in copies:
                copy.wait_recv()
        piece = panels.at[:, pl.ds(core * half, half)]
        copies = panel_start([(piece, piece, along(0, 1 - mine_digit[0]))])
        yield
        copies[0].wait_recv()
        prepare()
        yield

    energy_copies = [
        make(eocc_ref, energies.at[occ], (send, recv), KINDS * CHUNKS, up),
        make(eocc_ref, energies.at[occ], (send, recv), KINDS * CHUNKS + 1, down),
        make(energies.at[below], energies.at[below], (send, recv), KINDS * CHUNKS + 2, up),
    ]

    def scatter(c):
        def one(n, _):
            q = lax.rem(plane + n, slabs)
            make(packed[c].at[level * slabs + q], near[c].at[plane], (xy_send, xy_recv), 2 * c, member(q)).start()
            make(packed[c].at[(1 - level) * slabs + q], away[c].at[plane], (xy_send, xy_recv), 2 * c + 1,
                 member(q)).start()
            return 0

        lax.fori_loop(1, slabs, one, 0)
        own_of(c, 0).start()
        own_of(c, 1).start()
        if c + 1 < CHUNKS:
            pack(c + 1)

    def own_of(c, which):
        if which == 0:
            return pltpu.make_async_copy(packed[c].at[level * slabs + plane], near[c].at[plane], own_sem.at[1 + 2 * c])
        return pltpu.make_async_copy(packed[c].at[(1 - level) * slabs + plane], away[c].at[plane], own_sem.at[2 + 2 * c])

    def whole(ref, count, sem):
        at = ref.at[pl.ds(0, count)]
        return pltpu.make_async_copy(at, at, sem)

    def flips(c):
        count = slabs // 2
        source = away[c]
        return [
            make(source.at[pl.ds(n * count, count)], near[c].at[pl.ds(slabs + n * count, count)],
                 (flip_send, flip_recv), 2 * c + n, peer)
            for n, peer in enumerate((inside, across))
        ]

    def exchange(c, kind):
        sems, at = (send, recv), KINDS * c + kind
        group = lambda shift: pl.ds(lax.rem(occ + N_OCC + shift, N_OCC) * share, share)
        if kind == 0:
            return make(compact.at[c, group(0)], held.at[c, 0, occ], sems, at, up)
        if kind == 1:
            return make(compact.at[c, group(1)], held.at[c, 1, occ], sems, at, down)
        if kind == 2:
            return make(compact.at[c, group(-1)], held.at[c, 1, occ], sems, at, up)
        if kind == 3:
            return make(compact.at[c, group(-2)], held.at[c, 0, occ], sems, at, down)
        if kind == 4:
            return make(held.at[c, 0, below], held.at[c, 1, below], sems, at, up)
        if kind == 5:
            return make(held.at[c, 1, above], held.at[c, 0, above], sems, at, down)
        if kind == 6:
            return make(result.at[c, 0], out_ref.at[c, group(-1)], sems, at, down)
        return make(result.at[c, 1], out_ref.at[c, group(-2)], sems, at, up)

    def gather(c):
        whole(away[c], slabs - 1, xy_recv.at[2 * c + 1]).wait()
        own_of(c, 1).wait()
        for copy in flips(c):
            copy.start()
        whole(near[c], slabs - 1, xy_recv.at[2 * c]).wait()
        own_of(c, 0).wait()

    def select(c):
        for copy in flips(c):
            copy.wait_recv()

        def one(p, _):
            slab = near[c][slot_ref[p]]
            compact[c, p] = slab[:rows]
            if c == 0:
                eps_ref[p] = slab[rows : rows + 8]
            return 0

        lax.fori_loop(0, pairs, one, 0)
        for kind in range(2):
            exchange(c, kind).start()

    def direct(c):
        for kind in range(2, 4):
            exchange(c, kind).start()

        def keep(p, _):
            for role in range(2):
                held[c, role, occ, p] = compact[c, lax.rem(occ + N_OCC - 1 - role, N_OCC) * share + p]
            return 0

        lax.fori_loop(0, share, keep, 0)

    def relay(c):
        for n in range(2):
            exchange(c, n).wait_recv()
            exchange(c, 4 + n).start()

    def prepare():
        for n in range(N_OCC):
            pieces = ((n * depth, n * LANES, LANES), (n * depth + LANES, N_OCC * LANES + n * (depth - LANES), depth - LANES))
            for origin, target, count in pieces:
                for o in range(N_OCC):
                    stacked = panels[o, origin // 8 * across_units : (origin + count) // 8 * across_units]
                    stacked = stacked.reshape(count // 8, across_units, 8, LANES)
                    for k in range(across_units):
                        value = stacked[:, k].reshape(count, LANES)
                        upper = value.astype(jnp.bfloat16)
                        at = slice(k * LANES, (k + 1) * LANES)
                        high[o, target : target + count, at] = upper
                        low[o, target : target + count, at] = (value - upper.astype(jnp.float32)).astype(jnp.bfloat16)

    def compute(c):
        for kind in range(2, 6):
            exchange(c, kind).wait_recv()
        low_lane = lax.broadcasted_iota(jnp.int32, (fine, LANES), 1) < LANES // 2

        def arrange(q, _):
            role, p = q // share, q % share
            number = lax.rem(occ + N_OCC - 1 - role, N_OCC) * share + p
            turned = slot_ref[number] >= slabs + slabs // 2
            value = [
                jnp.where(turned, held[c, role, lax.rem(n + N_OCC - turn, N_OCC), p], held[c, role, n, p])
                for n in range(N_OCC)
            ]
            tiles = [v[: 2 * fine] for v in value]
            folds = [v[2 * fine :] for v in value]
            for n in range(0, N_OCC, 2):
                one = jnp.where(low_lane, folds[n], pltpu.roll(folds[n + 1], LANES // 2, 1))
                two = jnp.where(low_lane, pltpu.roll(folds[n], LANES // 2, 1), folds[n + 1])
                tiles.append(jnp.concatenate([one, two], axis=0))
            full = jnp.concatenate(tiles, axis=1)
            upper = full.astype(jnp.bfloat16)
            at = pl.ds(pl.multiple_of(q * 2 * fine, 16), 2 * fine)
            left_high[at] = upper
            left_low[at] = (full - upper.astype(jnp.float32)).astype(jnp.bfloat16)
            columns = eps_ref[number].T[c * fine : (c + 1) * fine]
            eps_col[at] = jnp.concatenate([columns[:, 0:1], columns[:, 1:2]], axis=0)
            return 0

        lax.fori_loop(0, 2 * share, arrange, 0)
        tall = share * 2 * fine
        for role, other_one in enumerate((below, above)):
            rows_of = pl.ds(role * tall, tall)
            for o in (other_one, occ):
                dot = lambda a, b: jnp.dot(a[rows_of], b[o], preferred_element_type=jnp.float32)
                total = (dot(left_high, low) + dot(left_low, high)) + dot(left_high, high)
                total = total / (eps_col[rows_of] - energies[o, 0:1])
                total = total.reshape(share, 2 * fine, width)
                if o is occ:
                    out_ref[c, pl.ds(lax.rem(occ + N_OCC - 1 - role, N_OCC) * share, share)] = total
                else:
                    result[c, role] = total
        for kind in range(6, 8):
            exchange(c, kind).start()

    for n in range(2):
        energy_copies[n].start()
    energies[occ] = eocc_ref[...]
    panel = panel_stages()
    steps = {"A": scatter, "B": gather, "S": select, "D": direct, "R": relay, "C": compute}
    for name in ORDER:
        if name == "P":
            next(panel, None)
            continue
        if name == "R0":
            for n in range(2):
                energy_copies[n].wait_recv()
            energy_copies[2].start()
        if name == "C0":
            energy_copies[2].wait_recv()
        steps[name[0]](int(name[1:]))

    for c in range(CHUNKS):
        for kind in range(6, 8):
            exchange(c, kind).wait_recv()
        for kind in range(KINDS):
            exchange(c, kind).wait_send()
        for copy in flips(c):
            copy.wait_send()
        whole(near[c], slabs - 1, xy_send.at[2 * c]).wait()
        whole(away[c], slabs - 1, xy_send.at[2 * c + 1]).wait()
    for copy in panel_copies + energy_copies:
        copy.wait_send()


def ladder_of(integrals, energies, amplitudes, eps_occ, panel_owner, slot_of, first, second, digits):
    blocks, lanes = energies.shape
    depth, col_count = integrals.shape
    slabs = first.shape[0] // 2
    pairs = slot_of.shape[0]
    panel_rows, width = amplitudes.shape
    share = pairs // N_OCC
    sizes = chunk_rows(col_count // blocks)
    rows = sizes[-1]
    fine = rows // 3
    f32, bf16 = jnp.float32, jnp.bfloat16
    vmem, dma = pl.BlockSpec(memory_space=pltpu.VMEM), pltpu.SemaphoreType.DMA
    smem = pl.BlockSpec(memory_space=pltpu.SMEM)
    units = (panel_rows // 8) * (width // lanes)
    amps = amplitudes.reshape(panel_rows // 8, 8, width // lanes, lanes).transpose(0, 2, 1, 3).reshape(units, 8, lanes)
    arrived, kept, length, count = [], [], units, 2 * N_OCC
    for n, (_, size) in enumerate(digits):
        length //= size
        arrived.append(pltpu.VMEM((size - 1, length, 8, lanes), f32))
        kept.append(pltpu.VMEM((length, 8, lanes), f32))
        count += (size - 1) * (2 if n > 1 else 1)
    return pl.pallas_call(
        functools.partial(ladder_kernel, digits),
        out_shape=jax.ShapeDtypeStruct((CHUNKS, pairs, 2 * fine, width), f32),
        in_specs=[smem] * 4 + [vmem] * 4,
        out_specs=vmem,
        scratch_shapes=[pltpu.VMEM((count_of, size, lanes), f32) for count_of in (2 * slabs, slabs, 2 * slabs) for size in sizes]
        + arrived
        + kept[:-1]
        + [
            pltpu.VMEM((col_count // 8, 8, 2 * lanes), f32),
            pltpu.VMEM((CHUNKS, pairs, rows, lanes), f32),
            pltpu.VMEM((CHUNKS, 2, N_OCC, share, rows, lanes), f32),
            pltpu.VMEM((CHUNKS, 2, share, 2 * fine, width), f32),
            pltpu.VMEM((N_OCC, units, 8, lanes), f32),
            pltpu.VMEM((N_OCC, panel_rows, width), bf16),
            pltpu.VMEM((N_OCC, panel_rows, width), bf16),
            pltpu.VMEM((share * 4 * fine, panel_rows), bf16),
            pltpu.VMEM((share * 4 * fine, panel_rows), bf16),
            pltpu.VMEM((pairs, 8, lanes), f32),
            pltpu.VMEM((share * 4 * fine, 1), f32),
            pltpu.VMEM((N_OCC, 1, width), f32),
            dma((2 * CHUNKS,)),
            dma((2 * CHUNKS,)),
            dma((1 + 2 * CHUNKS,)),
            dma((2 * CHUNKS,)),
            dma((2 * CHUNKS,)),
            dma((KINDS * CHUNKS + 3,)),
            dma((KINDS * CHUNKS + 3,)),
            dma((count,)),
            dma((count,)),
        ],
        compiler_params=pltpu.CompilerParams(collective_id=1, has_side_effects=True, vmem_limit_bytes=63 * 2**20),
        name="ladder",
    )(slot_of, panel_owner, first, second, integrals, energies[:, None], amps, eps_occ[None, :])


def local(amplitudes, integrals, eps_vir, eps_occ, panel_owner, block_target):
    me = lax.axis_index("vir")
    senders = lax.axis_size("vir")
    depth, col_count = integrals.shape
    blocks_dev = block_target.shape[0] // senders
    block = col_count // blocks_dev
    stride, levels = DIGITS[1]
    inner = stride
    slabs = senders // levels

    owners = block_target.reshape(senders, blocks_dev) // blocks_dev
    position = jnp.arange(blocks_dev, dtype=jnp.int32)
    order = jnp.arange(senders, dtype=jnp.int32)
    dest = order % slabs
    dest = (dest // inner) * (levels * inner) + (order // slabs) * inner + dest % inner
    goes = lax.dynamic_index_in_dim(owners, me, 0, keepdims=False)[None, :] == dest[:, None]
    first = jnp.min(jnp.where(goes, position[None, :], blocks_dev - 1), axis=1)
    second = jnp.max(jnp.where(goes, position[None, :], 0), axis=1)

    comes = owners == me
    sends = jnp.any(comes, axis=1)
    level = (order // inner) % levels
    slot = (order // (levels * inner)) * inner + order % inner
    slot = slot + jnp.where(level == (me // inner) % levels, 0, slabs)
    rank = jnp.sum((sends[None, :] & (slot[None, :] < slot[:, None])).astype(jnp.int32), axis=1)
    pair = jnp.arange(senders // 2, dtype=jnp.int32)
    slot_of = jnp.sum(jnp.where(sends[None, :] & (rank[None, :] == pair[:, None]), slot[None, :], 0), axis=1)
    lead = jnp.min(jnp.where(comes, position[None, :], blocks_dev), axis=1)
    stands = 2 * rank[:, None] + (position[None, :] != lead[:, None]).astype(jnp.int32)
    wanted = me * blocks_dev + position
    found = block_target.reshape(1, senders, blocks_dev) == wanted[:, None, None]
    source = jnp.sum(jnp.where(found, stands[None], 0), axis=(1, 2))

    energies = jnp.pad(eps_vir.reshape(blocks_dev, block), ((0, 0), (0, LANES - block)))
    ladder = ladder_of(
        integrals, energies, amplitudes, eps_occ, panel_owner, slot_of, first, second, DIGITS
    )
    return place(ladder, source)


def solution(mesh):
    in_specs = (P("vir", "occ"), P("occ", "vir"), P("vir"), P("occ"), P(), P())
    out_specs = P("vir", "occ")
    return jax.shard_map(local, mesh=mesh, in_specs=in_specs, out_specs=out_specs, check_vma=False)
```
